128 devices in a mesh: sector: 16 (over z, y), ops: 8 (over x, core).
Axes of the slice: x: 4, y: 4, z: 4, core: 2. Of those that a mesh axis runs over, the one named last changes fastest.
Arguments:
- wavefunction: float32 [16, 640, 640], P('sector'), may hold values from -160 to 160
- left_env: float32 [16, 32, 640, 640], P('sector', 'ops'), may hold values from -0.25 to 0.25
- right_env: float32 [16, 32, 640, 640], P('sector', 'ops'), may hold values from -0.25 to 0.25
- shift_map: int32 [8, 16], P('ops'), may hold values from 0 to 15, each once within a row
- op_counts: int32 [8, 16], P('ops', 'sector'), may hold values from 1 to 4
Outputs:
- updated_tensor: float32 [16, 640, 640], P('sector', None, 'ops')
- rotated_env: float32 [16, 32, 640, 640], P('sector', 'ops')
The draws below stay inside these ranges and needn't reach their ends.
Inputs may be any that keep to these rules, and one draw needn't show every extreme that they name: `shift_map`: each row lists every sector once.
All inputs are finite; a program needn't handle non-finite values.
Results may differ from the reference program's by a relative error of at most 0.0003.
Values sent between devices are 32-bit elements; how exact they have to be, the bound alone decides.
No kernel may reach another device: no remote copies, remote signals or barrier semaphores. Data moves between devices by JAX's collectives and lax.ppermute only.
A program may use at most 128 MiB of HBM per device.

```python
import math
import jax
import jax.numpy as jnp
from jax import lax

MS = 640
OPS_DEV = 4
POLAR = 5
NSEC = 16
GROUPS = 8
OPS = 32


def draw_wavefunction(key, part):
    key_base = jax.random.fold_in(key, 11)
    sector_level = jnp.arange(NSEC, dtype=jnp.float32) / float(NSEC - 1)
    base_draw = jnp.clip(jax.random.normal(key_base, (NSEC, MS, MS), jnp.float32), -6.0, 6.0)
    sector_scale = 3.0 ** sector_level
    return base_draw * sector_scale[:, None, None]


def touch_ends(entries, rng, smallest, high):
    spot = [jax.random.randint(jax.random.fold_in(rng, axis), (), 0, length) for axis, length in enumerate(entries.shape)]
    main_axis = entries.shape.index(max(entries.shape))
    next_to = spot[:main_axis] + [(spot[main_axis] + 1) % entries.shape[main_axis]] + spot[main_axis + 1:]
    return entries.at[tuple(spot)].set(smallest).at[tuple(next_to)].set(high)


def levels(stream_key, extent, cuts, least, top_value):
    level = 1.0
    for dim, shards_of in cuts:
        heights = jax.random.uniform(jax.random.fold_in(jax.random.fold_in(stream_key, 6), dim), (shards_of,), jnp.float32, least / len(cuts), top_value / len(cuts))
        level = level * jnp.repeat(jnp.exp(heights), extent[dim] // shards_of).reshape((-1,) + (1,) * (len(extent) - 1 - dim))
    return level


def scatter_about(rng, dims, deviation, limit, cuts=(), kind=jnp.bfloat16):
    result = deviation * jax.random.normal(rng, dims, jnp.float32)
    if cuts:
        result = result * levels(rng, dims, cuts, -0.22, 0.18)
    return jnp.clip(result, -limit, limit).astype(kind)


def setup_inputs(seed: int = 0) -> dict:
    seeds = jax.random.split(jax.random.key(seed), 6)
    wavefunction = draw_wavefunction(jax.random.fold_in(seeds[5], 71), 0)
    left_env = scatter_about(seeds[1], (NSEC, OPS, MS, MS), MS ** -0.5, 0.25, ((0, 16), (1, 8)), jnp.float32)
    right_env = scatter_about(seeds[2], (NSEC, OPS, MS, MS), MS ** -0.5, 0.25, ((0, 16), (1, 8)), jnp.float32)
    shift_map = jax.vmap(lambda own: jax.random.permutation(own, NSEC))(jax.random.split(seeds[3], GROUPS)).reshape((GROUPS, NSEC)).astype(jnp.int32)
    op_counts = touch_ends(jax.random.randint(seeds[4], (GROUPS, NSEC), 1, OPS_DEV + 1), jax.random.fold_in(seeds[4], 1), 1, OPS_DEV).astype(jnp.int32)
    return {"wavefunction": wavefunction, "left_env": left_env, "right_env": right_env, "shift_map": shift_map, "op_counts": op_counts}


precise = lax.Precision.HIGHEST

def reference(wavefunction, left_env, right_env, shift_map, op_counts):
    sector_ids = jnp.arange(NSEC, dtype=jnp.int32)
    slots = jnp.arange(OPS, dtype=jnp.int32) % OPS_DEV

    def sector_sigma(sector_id):
        sources = shift_map[:, sector_id]
        blocks = jnp.repeat(wavefunction[sources], OPS_DEV, axis=0)
        limits = jnp.repeat(op_counts[:, sector_id], OPS_DEV, axis=0)
        active = (slots < limits).astype(jnp.float32)
        left_psi = jnp.einsum('wab,wbc->wac', left_env[sector_id], blocks, precision=precise)
        op_terms = jnp.einsum('wac,wcd->wad', left_psi, right_env[sector_id], precision=precise)
        return jnp.einsum('w,wad->ad', active, op_terms, precision=precise)
    sigma = lax.map(sector_sigma, sector_ids)
    mean_sq = lax.optimization_barrier(jnp.sum(sigma * sigma, axis=(1, 2))) / float(MS * MS)
    factor = lax.rsqrt(MS * mean_sq + 1e-06) / 2.2
    iterate = sigma * factor[:, None, None]
    for repeat_index in range(POLAR):
        gram_matrix = jnp.einsum('sab,scb->sac', iterate, iterate, precision=precise)
        iterate = 1.5 * iterate - 0.5 * jnp.einsum('sac,scb->sab', gram_matrix, iterate, precision=precise)
    updated = iterate * math.sqrt(MS)

    def rotate(sector_id):
        sources = shift_map[:, sector_id]
        rights = jnp.repeat(updated[sources], OPS_DEV, axis=0)
        half_rotated = jnp.einsum('ba,wbc->wac', updated[sector_id], left_env[sector_id], precision=precise)
        return jnp.einsum('wac,wcd->wad', half_rotated, rights, precision=precise)
    rotated = lax.map(rotate, sector_ids)
    return (updated, rotated)
```

```python
import math

import jax
import jax.numpy as jnp
from jax import lax
from jax.sharding import PartitionSpec as P

POLAR = 5
split = lax.Precision.HIGH


def mm(a, b):
    return jnp.dot(a, b, precision=split, preferred_element_type=jnp.float32)


def swap_cores(block, devices):
    return lax.ppermute(block, "ops", [(j, j ^ 1) for j in range(devices)])


def to_right(block, devices):
    return lax.ppermute(block, "ops", [(j, (j + 2) % devices) for j in range(devices)])


def to_left(block, devices):
    return lax.ppermute(block, "ops", [(j, (j - 2) % devices) for j in range(devices)])


def sum_over_ops(partial):
    devices = lax.axis_size("ops")
    chips = devices // 2
    here = lax.axis_index("ops")
    chip, core = here // 2, here % 2
    half = partial.shape[0] // 2
    rows = half // chips
    mid = rows // 2

    def rows_at(block, index, count):
        return lax.dynamic_slice_in_dim(block, index * count, count, 0)

    pair = rows_at(partial, core, half) + swap_cores(rows_at(partial, 1 - core, half), devices)
    right, left, far = (chip + 1) % chips, (chip + 3) % chips, (chip + 2) % chips
    far_rows = rows_at(pair, far, rows)
    from_left = to_right(far_rows[:mid], devices)
    from_right = to_left(far_rows[mid:], devices)
    right_rows, left_rows = rows_at(pair, right, rows), rows_at(pair, left, rows)
    right_rows = jnp.concatenate([right_rows[:mid] + from_left, right_rows[mid:]], 0)
    left_rows = jnp.concatenate([left_rows[:mid], left_rows[mid:] + from_right], 0)
    own = rows_at(pair, chip, rows) + to_right(right_rows, devices) + to_left(left_rows, devices)

    from_left, from_right = to_right(own, devices), to_left(own, devices)
    far_first = to_right(from_left[:mid], devices)
    far_second = to_left(from_right[mid:], devices)
    ring = jnp.concatenate([own, from_right, far_first, far_second, from_left] * 2, 0)
    mine = lax.dynamic_slice_in_dim(ring, ((chips - chip) % chips) * rows, half, 0)
    other = swap_cores(mine, devices)
    both = jnp.concatenate([mine, other, mine], 0)
    return lax.dynamic_slice_in_dim(both, core * half, 2 * half, 0)


def fetch_block(block, sources):
    sectors = lax.axis_size("sector")
    devices = lax.axis_size("ops")
    core = lax.axis_index("ops") % 2
    states = block.shape[0]
    rows = states // sectors
    part = (rows // 2 + 7) // 8 * 8
    pieces = block.reshape(sectors, rows, states)
    own_part = lax.dynamic_slice_in_dim(pieces, core * (rows - part), part, 1)
    spread = lax.all_to_all(own_part, "sector", split_axis=0, concat_axis=0, tiled=True)
    sibling = swap_cores(spread, devices)
    first = jnp.where(core == 0, spread, sibling)
    second = jnp.where(core == 0, sibling, spread)
    whole = jnp.concatenate([first, second[:, 2 * part - rows :]], 1)
    picked = jnp.take(whole, sources, axis=0)
    return lax.all_to_all(picked, "sector", split_axis=0, concat_axis=0, tiled=True).reshape(states, states)


def shards(wavefunction, left_env, right_env, shift_map, op_counts):
    group_size = lax.axis_size("ops")
    group_here = lax.axis_index("ops")
    states = wavefunction.shape[1]
    sources = shift_map[0]
    moved_block = fetch_block(wavefunction[0], sources)

    def add_term(op_index, running):
        left_block = lax.dynamic_index_in_dim(left_env[0], op_index, 0, keepdims=False)
        right_block = lax.dynamic_index_in_dim(right_env[0], op_index, 0, keepdims=False)
        return running + mm(mm(left_block, moved_block), right_block)

    partial_sigma = lax.fori_loop(0, op_counts[0, 0], add_term, jnp.zeros((states, states), jnp.float32))
    sigma_block = sum_over_ops(partial_sigma)
    mean_sq = jnp.sum(sigma_block * sigma_block) / float(states * states)
    iterate = sigma_block * (lax.rsqrt(states * mean_sq + 1e-06) / 2.2)
    for _ in range(POLAR):
        gram_matrix = mm(iterate, iterate.T)
        iterate = 1.5 * iterate - 0.5 * mm(gram_matrix, iterate)
    whole_tensor = iterate * math.sqrt(states)
    column_width = states // group_size
    own_columns = lax.dynamic_slice_in_dim(whole_tensor, group_here * column_width, column_width, 1)
    source_tensor = fetch_block(whole_tensor, sources)
    half_rotated = jnp.einsum("ba,wbc->wac", whole_tensor, left_env[0], precision=split)
    rotated = jnp.einsum("wac,cd->wad", half_rotated, source_tensor, precision=split)
    return (own_columns[None], rotated[None])


def solution(mesh):
    return jax.shard_map(
        shards,
        mesh=mesh,
        in_specs=(
            P("sector", None, None),
            P("sector", "ops", None, None),
            P("sector", "ops", None, None),
            P("ops", None),
            P("ops", "sector"),
        ),
        out_specs=(P("sector", None, "ops"), P("sector", "ops", None, None)),
        check_vma=False,
    )
```

```python
import functools
import math

import jax
import jax.numpy as jnp
from jax import lax
from jax.experimental import pallas as pl
from jax.experimental.pallas import tpu as pltpu
from jax.sharding import Mesh
from jax.sharding import PartitionSpec as P

POLAR = 5
F32, BF16 = jnp.float32, jnp.bfloat16
VMEM_LIMIT = 48 << 20
WHOLE = pl.BlockSpec(memory_space=pltpu.VMEM)


def halves(v):
    high = v.astype(BF16)
    return high, (v - high.astype(F32)).astype(BF16)


def side_by_side(ref, a, b, c):
    n = a.shape[1]
    ref[:, 0:n] = a
    ref[:, n : 2 * n] = b
    ref[:, 2 * n : 3 * n] = c


def stacked(ref, a, b, c):
    n = a.shape[0]
    ref[0:n] = a
    ref[n : 2 * n] = b
    ref[2 * n : 3 * n] = c


def left_form(ref, v):
    high, low = halves(v)
    side_by_side(ref, high, high, low)


def right_form(ref, v):
    high, low = halves(v)
    stacked(ref, high, low, high)


def mm(a, b):
    return jnp.dot(a, b, preferred_element_type=F32)


def mm_nt(a, b):
    return lax.dot_general(a, b, (((1,), (1,)), ((), ())), preferred_element_type=F32)


def params():
    return pltpu.CompilerParams(vmem_limit_bytes=VMEM_LIMIT)


def cost(flops, nbytes):
    return pl.CostEstimate(flops=int(flops), bytes_accessed=int(nbytes), transcendentals=0)


def prepare_kernel(l_ref, r_ref, lo_ref, ro_ref):
    left_form(lo_ref.at[0], l_ref[0])
    right_form(ro_ref.at[0], r_ref[0])


def prepare(left, right):
    k, n, _ = left.shape
    block = pl.BlockSpec((1, n, n), lambda w: (w, 0, 0))
    return pl.pallas_call(
        prepare_kernel,
        grid=(k,),
        out_shape=(jax.ShapeDtypeStruct((k, n, 3 * n), BF16), jax.ShapeDtypeStruct((k, 3 * n, n), BF16)),
        in_specs=[block, block],
        out_specs=(pl.BlockSpec((1, n, 3 * n), lambda w: (w, 0, 0)), pl.BlockSpec((1, 3 * n, n), lambda w: (w, 0, 0))),
        compiler_params=params(),
        cost_estimate=cost(8 * k * n * n, 20 * k * n * n),
        name="prepare",
    )(left, right)


def sigma_kernel(scalars, w_ref, l_ref, r_ref, own_ref, other_ref, w3, mid, acc):
    step = pl.program_id(0)
    half = own_ref.shape[0]

    @pl.when(step == 0)
    def _():
        right_form(w3, w_ref[...])

    @pl.when(step < scalars[0])
    def _():
        left_form(mid, mm(l_ref[0], w3[...]))
        term = mm(mid[...], r_ref[0])

        @pl.when(step == 0)
        def _():
            acc[...] = term

        @pl.when(step > 0)
        def _():
            acc[...] += term

    @pl.when(step == pl.num_programs(0) - 1)
    def _():
        core = scalars[1]
        own_ref[...] = acc[pl.ds(pl.multiple_of(core * half, half), half)]
        other_ref[...] = acc[pl.ds(pl.multiple_of((1 - core) * half, half), half)]


def partial_sigma(scalars, block, left3, right3):
    k, n = left3.shape[0], block.shape[0]
    half = n // 2

    def active(w, s):
        return (jnp.minimum(w, s[0] - 1), 0, 0)

    return pl.pallas_call(
        sigma_kernel,
        out_shape=(jax.ShapeDtypeStruct((half, n), F32),) * 2,
        grid_spec=pltpu.PrefetchScalarGridSpec(
            num_scalar_prefetch=1,
            grid=(k,),
            in_specs=[
                pl.BlockSpec((n, n), lambda w, s: (0, 0)),
                pl.BlockSpec((1, n, 3 * n), active),
                pl.BlockSpec((1, 3 * n, n), active),
            ],
            out_specs=(pl.BlockSpec((half, n), lambda w, s: (0, 0)),) * 2,
            scratch_shapes=[pltpu.VMEM((3 * n, n), BF16), pltpu.VMEM((n, 3 * n), BF16), pltpu.VMEM((n, n), F32)],
        ),
        compiler_params=params(),
        cost_estimate=cost(12 * k * n**3, 16 * k * n * n),
        name="partial_sigma",
    )(scalars, block, left3, right3)


def polar_kernel(core_ref, mine_ref, other_ref, u_ref, ut_ref, x, a, b, r):
    n = x.shape[0]
    half = n // 2
    core = core_ref[0]
    mine, other = mine_ref[...], other_ref[...]
    mean_sq = (jnp.sum(mine * mine) + jnp.sum(other * other)) / float(n * n)
    factor = lax.rsqrt(n * mean_sq + 1e-06) / 2.2
    x[pl.ds(pl.multiple_of(core * half, half), half)] = mine * factor
    x[pl.ds(pl.multiple_of((1 - core) * half, half), half)] = other * factor

    def iteration(_, carry):
        high, low = halves(x[...])
        side_by_side(a, high, high, low)
        side_by_side(b, high, low, high)
        stacked(r, high, low, high)
        first = mm_nt(a[...], b[0:256])
        second = mm_nt(a[256:n], b[256:512])
        third = mm_nt(a[512:n], b[512:n])
        rows = (
            (0, (first[0:256], first[256:n].T)),
            (256, (first[256:512], second[0:256], second[256 : n - 256].T)),
            (512, (first[512:n], second[256 : n - 256], third)),
        )
        for start, blocks in rows:
            high, low = halves(jnp.concatenate(blocks, 1))
            side_by_side(a.at[start : start + high.shape[0]], high, high, low)
        x[...] = 1.5 * x[...] - 0.5 * mm(a[...], r[...])
        return carry

    lax.fori_loop(0, POLAR, iteration, 0)
    updated = x[...] * math.sqrt(n)
    u_ref[...] = updated
    left_form(ut_ref, updated.T)


def polar(core, mine, other):
    n = mine.shape[1]
    return pl.pallas_call(
        polar_kernel,
        out_shape=(jax.ShapeDtypeStruct((n, n), F32), jax.ShapeDtypeStruct((n, 3 * n), BF16)),
        in_specs=[pl.BlockSpec(memory_space=pltpu.SMEM), WHOLE, WHOLE],
        out_specs=(WHOLE, WHOLE),
        scratch_shapes=[
            pltpu.VMEM((n, n), F32),
            pltpu.VMEM((n, 3 * n), BF16),
            pltpu.VMEM((n, 3 * n), BF16),
            pltpu.VMEM((3 * n, n), BF16),
        ],
        compiler_params=params(),
        cost_estimate=cost(POLAR * 12 * n**3, 14 * n * n),
        name="polar",
    )(core, mine, other)


def half_kernel(ut_ref, l_ref, o_ref, l3):
    right_form(l3, l_ref[0])
    left_form(o_ref.at[0], mm(ut_ref[...], l3[...]))


def half_rotated(ut3, left):
    k, n, _ = left.shape
    return pl.pallas_call(
        half_kernel,
        grid=(k,),
        out_shape=jax.ShapeDtypeStruct((k, n, 3 * n), BF16),
        in_specs=[pl.BlockSpec((n, 3 * n), lambda w: (0, 0)), pl.BlockSpec((1, n, n), lambda w: (w, 0, 0))],
        out_specs=pl.BlockSpec((1, n, 3 * n), lambda w: (w, 0, 0)),
        scratch_shapes=[pltpu.VMEM((3 * n, n), BF16)],
        compiler_params=params(),
        cost_estimate=cost(6 * k * n**3, 10 * k * n * n),
        name="half_rotated",
    )(ut3, left)


def rotate_kernel(h_ref, u_ref, o_ref, u3):
    @pl.when(pl.program_id(0) == 0)
    def _():
        right_form(u3, u_ref[...])

    o_ref[0] = mm(h_ref[0], u3[...])


def rotate(half3, source):
    k, n = half3.shape[0], source.shape[0]
    return pl.pallas_call(
        rotate_kernel,
        grid=(k,),
        out_shape=jax.ShapeDtypeStruct((k, n, n), F32),
        in_specs=[pl.BlockSpec((1, n, 3 * n), lambda w: (w, 0, 0)), pl.BlockSpec((n, n), lambda w: (0, 0))],
        out_specs=pl.BlockSpec((1, n, n), lambda w: (w, 0, 0)),
        scratch_shapes=[pltpu.VMEM((3 * n, n), BF16)],
        compiler_params=params(),
        cost_estimate=cost(6 * k * n**3, 10 * k * n * n),
        name="rotate",
    )(half3, source)


def fetch_block(block, sources):
    sectors, states = lax.axis_size("sector"), block.shape[0]
    pieces = block.reshape(sectors, states // sectors, states)
    spread = lax.all_to_all(pieces, "sector", split_axis=0, concat_axis=0, tiled=True)
    picked = jnp.take(spread, sources, axis=0, mode="clip")
    return lax.all_to_all(picked, "sector", split_axis=0, concat_axis=0, tiled=True).reshape(states, states)


def swap_cores(block):
    return lax.ppermute(block, "core", [(0, 1), (1, 0)])


def shards(wavefunction, left_env, right_env, shift_map, op_counts):
    chips = lax.axis_size("x")
    core = lax.axis_index("core")
    group_size = chips * lax.axis_size("core")
    group_here = lax.axis_index("x") * lax.axis_size("core") + core
    states = wavefunction.shape[1]
    half = states // 2
    sources = shift_map[0]
    left3, right3 = prepare(left_env[0], right_env[0])
    moved_block = fetch_block(wavefunction[0], sources)

    scalars = jnp.stack([op_counts[0, 0], core.astype(jnp.int32)])
    own, other = partial_sigma(scalars, moved_block, left3, right3)
    pair = (own + swap_cores(other)).reshape(chips, half // chips, states)
    rows = jnp.sum(lax.all_to_all(pair, "x", split_axis=0, concat_axis=0, tiled=True), axis=0)
    mine = lax.all_gather(rows, "x", tiled=True)
    updated, ut3 = polar(scalars[1:], mine, swap_cores(mine))

    column_width = states // group_size
    own_columns = lax.dynamic_slice_in_dim(updated, group_here * column_width, column_width, 1)
    source_tensor = fetch_block(updated, sources)
    rotated = rotate(half_rotated(ut3, left_env[0]), source_tensor)
    return (own_columns[None], rotated[None])


def solution(mesh):
    sectors, groups = mesh.devices.shape
    fine = Mesh(mesh.devices.reshape(sectors, groups // 2, 2), ("sector", "x", "core"))
    ops = ("x", "core")
    return jax.shard_map(
        shards,
        mesh=fine,
        in_specs=(
            P("sector", None, None),
            P("sector", ops, None, None),
            P("sector", ops, None, None),
            P(ops, None),
            P(ops, "sector"),
        ),
        out_specs=(P("sector", None, ops), P("sector", ops, None, None)),
        check_vma=False,
    )
```

```python
import functools
import math

import jax
import jax.numpy as jnp
from jax import lax
from jax.experimental import pallas as pl
from jax.experimental.pallas import tpu as pltpu
from jax.sharding import Mesh
from jax.sharding import PartitionSpec as P

POLAR = 5
SECTORS = 16
LANES = 128
F32, BF16 = jnp.float32, jnp.bfloat16
VMEM_LIMIT = 48 << 20
WHOLE = pl.BlockSpec(memory_space=pltpu.VMEM)


def halves(v):
    high = v.astype(BF16)
    return high, (v - high.astype(F32)).astype(BF16)


def side_by_side(ref, a, b, c):
    n = a.shape[1]
    ref[:, 0:n] = a
    ref[:, n : 2 * n] = b
    ref[:, 2 * n : 3 * n] = c


def stacked(ref, a, b, c):
    n = a.shape[0]
    ref[0:n] = a
    ref[n : 2 * n] = b
    ref[2 * n : 3 * n] = c


def left_form(ref, v):
    high, low = halves(v)
    side_by_side(ref, high, high, low)


def right_form(ref, v):
    high, low = halves(v)
    stacked(ref, high, low, high)


def mm(a, b):
    return jnp.dot(a, b, preferred_element_type=F32)


def mm_nt(a, b):
    return lax.dot_general(a, b, (((1,), (1,)), ((), ())), preferred_element_type=F32)


def params():
    return pltpu.CompilerParams(vmem_limit_bytes=VMEM_LIMIT)


def cost(flops, nbytes):
    return pl.CostEstimate(flops=int(flops), bytes_accessed=int(nbytes), transcendentals=0)


def prepare_kernel(l_ref, r_ref, lo_ref, ro_ref):
    left_form(lo_ref.at[0], l_ref[0])
    right_form(ro_ref.at[0], r_ref[0])


def prepare(left, right):
    k, n, _ = left.shape
    block = pl.BlockSpec((1, n, n), lambda w: (w, 0, 0))
    return pl.pallas_call(
        prepare_kernel,
        grid=(k,),
        out_shape=(jax.ShapeDtypeStruct((k, n, 3 * n), BF16), jax.ShapeDtypeStruct((k, 3 * n, n), BF16)),
        in_specs=[block, block],
        out_specs=(pl.BlockSpec((1, n, 3 * n), lambda w: (w, 0, 0)), pl.BlockSpec((1, 3 * n, n), lambda w: (w, 0, 0))),
        compiler_params=params(),
        cost_estimate=cost(8 * k * n * n, 20 * k * n * n),
        name="prepare",
    )(left, right)


def columns_to_rows(ref, v):
    n = v.shape[0]
    for t in range(n // LANES):
        ref[t * n : (t + 1) * n] = v[:, t * LANES : (t + 1) * LANES]


def halves_at(ref, core):
    half = ref.shape[0] // 2
    return (
        pl.ds(pl.multiple_of(core * half, half), half),
        pl.ds(pl.multiple_of((1 - core) * half, half), half),
    )


def sigma_kernel(scalars, w_ref, l_ref, r_ref, own_ref, other_ref, w3, mid, acc, rows):
    step = pl.program_id(0)
    n = acc.shape[0]

    @pl.when(step == 0)
    def _():
        pieces, count, _ = w_ref.shape
        chips = pieces // SECTORS
        for piece in range(pieces):
            start = (piece % chips * SECTORS + piece // chips) * count
            rows[start : start + count] = w_ref[piece]
        for t in range(n // LANES):
            high, low = halves(rows[t * n : (t + 1) * n])
            stacked(w3.at[:, t * LANES : (t + 1) * LANES], high, low, high)

    @pl.when(step < scalars[0])
    def _():
        left_form(mid, mm(l_ref[0], w3[...]))
        term = mm(mid[...], r_ref[0])

        @pl.when(step == 0)
        def _():
            acc[...] = term

        @pl.when(step > 0)
        def _():
            acc[...] += term

    @pl.when(step == pl.num_programs(0) - 1)
    def _():
        columns_to_rows(rows, acc)
        own, other = halves_at(rows, scalars[1])
        own_ref[...] = rows[own]
        other_ref[...] = rows[other]


def partial_sigma(scalars, pieces, left3, right3):
    k, n = left3.shape[:2]
    lines = n * n // LANES

    def active(w, s):
        return (jnp.minimum(w, s[0] - 1), 0, 0)

    return pl.pallas_call(
        sigma_kernel,
        out_shape=(jax.ShapeDtypeStruct((lines // 2, LANES), F32),) * 2,
        grid_spec=pltpu.PrefetchScalarGridSpec(
            num_scalar_prefetch=1,
            grid=(k,),
            in_specs=[
                pl.BlockSpec(pieces.shape, lambda w, s: (0, 0, 0)),
                pl.BlockSpec((1, n, 3 * n), active),
                pl.BlockSpec((1, 3 * n, n), active),
            ],
            out_specs=(pl.BlockSpec((lines // 2, LANES), lambda w, s: (0, 0)),) * 2,
            scratch_shapes=[
                pltpu.VMEM((3 * n, n), BF16),
                pltpu.VMEM((n, 3 * n), BF16),
                pltpu.VMEM((n, n), F32),
                pltpu.VMEM((lines, LANES), F32),
            ],
        ),
        compiler_params=params(),
        cost_estimate=cost(12 * k * n**3, 16 * k * n * n),
        name="partial_sigma",
    )(scalars, pieces, left3, right3)


def iterate_polar(rows, x, a, b, r):
    n = x.shape[0]
    mean_sq = jnp.sum(rows[...] * rows[...]) / float(n * n)
    factor = lax.rsqrt(n * mean_sq + 1e-06) / 2.2
    for t in range(n // LANES):
        x[:, t * LANES : (t + 1) * LANES] = rows[t * n : (t + 1) * n] * factor

    def iteration(_, carry):
        high, low = halves(x[...])
        side_by_side(a, high, high, low)
        side_by_side(b, high, low, high)
        stacked(r, high, low, high)
        first = mm_nt(a[...], b[0:256])
        second = mm_nt(a[256:n], b[256:512])
        third = mm_nt(a[512:n], b[512:n])
        blocks_of = (
            (0, (first[0:256], first[256:n].T)),
            (256, (first[256:512], second[0:256], second[256 : n - 256].T)),
            (512, (first[512:n], second[256 : n - 256], third)),
        )
        for start, blocks in blocks_of:
            high, low = halves(jnp.concatenate(blocks, 1))
            side_by_side(a.at[start : start + high.shape[0]], high, high, low)
        x[...] = 1.5 * x[...] - 0.5 * mm(a[...], r[...])
        return carry

    lax.fori_loop(0, POLAR, iteration, 0)


def polar_scratch(n):
    return [
        pltpu.VMEM((n * n // LANES, LANES), F32),
        pltpu.VMEM((n, n), F32),
        pltpu.VMEM((n, 3 * n), BF16),
        pltpu.VMEM((n, 3 * n), BF16),
        pltpu.VMEM((3 * n, n), BF16),
    ]


def own_polar_kernel(scalars, p_ref, columns_ref, ut_ref, rows, x, a, b, r):
    pieces, count, _ = p_ref.shape
    mine, other = halves_at(rows, scalars[0])
    for piece in range(pieces // 2):
        lines = pl.ds(piece * count, count)
        rows.at[mine][lines] = p_ref[2 * piece]
        rows.at[other][lines] = p_ref[2 * piece + 1]
    iterate_polar(rows, x, a, b, r)
    updated = (x[...] * math.sqrt(x.shape[0])).T
    left_form(ut_ref, updated)
    x[...] = updated
    width = columns_ref.shape[0]
    columns_ref[...] = x[pl.ds(pl.multiple_of(scalars[1] * width, width), width)]


def own_polar(scalars, pieces, n):
    return pl.pallas_call(
        own_polar_kernel,
        out_shape=(jax.ShapeDtypeStruct((n // pieces.shape[0], n), F32), jax.ShapeDtypeStruct((n, 3 * n), BF16)),
        in_specs=[pl.BlockSpec(memory_space=pltpu.SMEM), WHOLE],
        out_specs=(WHOLE, WHOLE),
        scratch_shapes=polar_scratch(n),
        compiler_params=params(),
        cost_estimate=cost(POLAR * 12 * n**3, 14 * n * n),
        name="own_polar",
    )(scalars, pieces)


def source_polar_kernel(core_ref, p_ref, u_ref, rows, x, a, b, r, mine_rows, other_rows):
    pieces, count, _ = p_ref.shape
    chips, part = pieces // SECTORS, count // 2
    for piece in range(pieces):
        start = (piece % chips * SECTORS + piece // chips) * part
        mine_rows[start : start + part] = p_ref[piece, 0:part]
        other_rows[start : start + part] = p_ref[piece, part:count]
    mine, other = halves_at(rows, core_ref[0])
    rows[mine] = mine_rows[...]
    rows[other] = other_rows[...]
    iterate_polar(rows, x, a, b, r)
    right_form(u_ref, x[...] * math.sqrt(x.shape[0]))


def source_polar(core, pieces, n):
    half_rows = pltpu.VMEM((n * n // LANES // 2, LANES), F32)
    return pl.pallas_call(
        source_polar_kernel,
        out_shape=jax.ShapeDtypeStruct((3 * n, n), BF16),
        in_specs=[pl.BlockSpec(memory_space=pltpu.SMEM), WHOLE],
        out_specs=WHOLE,
        scratch_shapes=polar_scratch(n) + [half_rows, half_rows],
        compiler_params=params(),
        cost_estimate=cost(POLAR * 12 * n**3, 10 * n * n),
        name="source_polar",
    )(core, pieces)


def half_kernel(ut_ref, l_ref, o_ref, l3):
    right_form(l3, l_ref[0])
    left_form(o_ref.at[0], mm(ut_ref[...], l3[...]))


def half_rotated(ut3, left):
    k, n, _ = left.shape
    return pl.pallas_call(
        half_kernel,
        grid=(k,),
        out_shape=jax.ShapeDtypeStruct((k, n, 3 * n), BF16),
        in_specs=[pl.BlockSpec((n, 3 * n), lambda w: (0, 0)), pl.BlockSpec((1, n, n), lambda w: (w, 0, 0))],
        out_specs=pl.BlockSpec((1, n, 3 * n), lambda w: (w, 0, 0)),
        scratch_shapes=[pltpu.VMEM((3 * n, n), BF16)],
        compiler_params=params(),
        cost_estimate=cost(6 * k * n**3, 10 * k * n * n),
        name="half_rotated",
    )(ut3, left)


def rotate_kernel(h_ref, u_ref, o_ref):
    o_ref[0] = mm(h_ref[0], u_ref[...])


def rotate(half3, source3):
    k, n, _ = half3.shape
    return pl.pallas_call(
        rotate_kernel,
        grid=(k,),
        out_shape=jax.ShapeDtypeStruct((k, n, n), F32),
        in_specs=[pl.BlockSpec((1, n, 3 * n), lambda w: (w, 0, 0)), pl.BlockSpec((3 * n, n), lambda w: (0, 0))],
        out_specs=pl.BlockSpec((1, n, n), lambda w: (w, 0, 0)),
        compiler_params=params(),
        cost_estimate=cost(6 * k * n**3, 10 * k * n * n),
        name="rotate",
    )(half3, source3)


def cut_kernel(chip_ref, w_ref, o_ref, rows, part):
    columns_to_rows(rows, w_ref)
    lines = part.shape[0]
    part[...] = rows[pl.ds(pl.multiple_of(chip_ref[0] * lines, lines), lines)]
    pieces, count, _ = o_ref.shape
    for piece in range(pieces):
        o_ref[piece] = part[piece * count : (piece + 1) * count]


def cut(chip, block, chips):
    n = block.shape[0]
    lines = n * n // LANES
    return pl.pallas_call(
        cut_kernel,
        out_shape=jax.ShapeDtypeStruct((SECTORS, lines // chips // SECTORS, LANES), F32),
        in_specs=[pl.BlockSpec(memory_space=pltpu.SMEM), WHOLE],
        out_specs=WHOLE,
        scratch_shapes=[pltpu.VMEM((lines, LANES), F32), pltpu.VMEM((lines // chips, LANES), F32)],
        compiler_params=params(),
        cost_estimate=cost(n * n, 5 * n * n),
        name="cut",
    )(chip, block)


def pair_kernel(mine_ref, other_ref, o_ref):
    pieces, count, _ = o_ref.shape
    part = count // 2
    for piece in range(pieces):
        lines = slice(piece * part, (piece + 1) * part)
        o_ref[piece, 0:part] = mine_ref[lines]
        o_ref[piece, part:count] = other_ref[lines]


def pair_up(mine, other):
    lines = mine.shape[0]
    return pl.pallas_call(
        pair_kernel,
        out_shape=jax.ShapeDtypeStruct((SECTORS, 2 * lines // SECTORS, LANES), F32),
        in_specs=[WHOLE, WHOLE],
        out_specs=WHOLE,
        compiler_params=params(),
        cost_estimate=cost(lines, 16 * lines * LANES),
        name="pair_up",
    )(mine, other)


def swap_cores(block):
    return lax.ppermute(block, "core", [(0, 1), (1, 0)])


def exchange(pieces, axes):
    return lax.all_to_all(pieces, axes, split_axis=0, concat_axis=0, tiled=True)


def fetch(pieces, readers):
    spread = exchange(pieces, "sector")
    return exchange(jnp.take(spread, readers, axis=0, mode="clip"), ("sector", "x"))


def shards(wavefunction, left_env, right_env, shift_map, op_counts):
    chips = lax.axis_size("x")
    chip, core = lax.axis_index("x"), lax.axis_index("core")
    group_here = chip * lax.axis_size("core") + core
    n = wavefunction.shape[1]
    lines = n * n // LANES
    scalars = jnp.stack([op_counts[0, 0], core.astype(jnp.int32)])
    readers = lax.all_gather(shift_map[0], "x").T.reshape(-1)
    left3, right3 = prepare(left_env[0], right_env[0])

    moved = fetch(cut(chip.astype(jnp.int32)[None], wavefunction[0], chips), readers)

    own, other = partial_sigma(scalars, moved, left3, right3)
    pair = (own + swap_cores(other)).reshape(chips, lines // 2 // chips, LANES)
    chunk = jnp.sum(exchange(pair, "x"), axis=0)

    other_chunk = swap_cores(chunk)
    source_pieces = fetch(pair_up(chunk, other_chunk), readers)

    own_pieces = lax.all_gather(jnp.stack([chunk, other_chunk]), "x", tiled=True)
    own_rows, ut3 = own_polar(jnp.stack([core, group_here]).astype(jnp.int32), own_pieces, n)
    half3, source_pieces = lax.optimization_barrier((half_rotated(ut3, left_env[0]), source_pieces))
    rotated = rotate(half3, source_polar(scalars[1:], source_pieces, n))
    return (own_rows.T[None], rotated[None])


def solution(mesh):
    sectors, groups = mesh.devices.shape
    fine = Mesh(mesh.devices.reshape(sectors, groups // 2, 2), ("sector", "x", "core"))
    ops = ("x", "core")
    return jax.shard_map(
        shards,
        mesh=fine,
        in_specs=(
            P("sector", None, None),
            P("sector", ops, None, None),
            P("sector", ops, None, None),
            P(ops, None),
            P(ops, "sector"),
        ),
        out_specs=(P("sector", None, ops), P("sector", ops, None, None)),
        check_vma=False,
    )
```

```python
import functools
import math

import jax
import jax.numpy as jnp
from jax import lax
from jax.experimental import pallas as pl
from jax.experimental.pallas import tpu as pltpu
from jax.sharding import Mesh
from jax.sharding import PartitionSpec as P

POLAR = 5
SECTORS = 16
GROUPS = 8
EARLY = 2
LANES = 128
F32, BF16 = jnp.float32, jnp.bfloat16
VMEM_LIMIT = 48 << 20
WHOLE = pl.BlockSpec(memory_space=pltpu.VMEM)


def halves(v):
    high = v.astype(BF16)
    return high, (v - high.astype(F32)).astype(BF16)


def side_by_side(ref, a, b, c):
    n = a.shape[1]
    ref[:, 0:n] = a
    ref[:, n : 2 * n] = b
    ref[:, 2 * n : 3 * n] = c


def stacked(ref, a, b, c):
    n = a.shape[0]
    ref[0:n] = a
    ref[n : 2 * n] = b
    ref[2 * n : 3 * n] = c


def left_form(ref, v):
    high, low = halves(v)
    side_by_side(ref, high, high, low)


def right_form(ref, v):
    high, low = halves(v)
    stacked(ref, high, low, high)


def mm(a, b):
    return jnp.dot(a, b, preferred_element_type=F32)


def mm_nt(a, b):
    return lax.dot_general(a, b, (((1,), (1,)), ((), ())), preferred_element_type=F32)


def params():
    return pltpu.CompilerParams(vmem_limit_bytes=VMEM_LIMIT)


def cost(flops, nbytes):
    return pl.CostEstimate(flops=int(flops), bytes_accessed=int(nbytes), transcendentals=0)


def prepare_kernel(l_ref, r_ref, lo_ref, ro_ref):
    left_form(lo_ref.at[0], l_ref[0])
    right_form(ro_ref.at[0], r_ref[0])


def prepare(left, right):
    k, n, _ = left.shape
    block = pl.BlockSpec((1, n, n), lambda w: (w, 0, 0))
    return pl.pallas_call(
        prepare_kernel,
        grid=(k,),
        out_shape=(jax.ShapeDtypeStruct((k, n, 3 * n), BF16), jax.ShapeDtypeStruct((k, 3 * n, n), BF16)),
        in_specs=[block, block],
        out_specs=(pl.BlockSpec((1, n, 3 * n), lambda w: (w, 0, 0)), pl.BlockSpec((1, 3 * n, n), lambda w: (w, 0, 0))),
        compiler_params=params(),
        cost_estimate=cost(8 * k * n * n, 20 * k * n * n),
        name="prepare",
    )(left, right)


def tiles(n):
    return [(t, slice(t * LANES, (t + 1) * LANES)) for t in range(n // LANES)]


def lines_of(ref, v):
    count = v.shape[0]
    for t, lanes in tiles(v.shape[1]):
        ref[t * count : (t + 1) * count] = v[:, lanes]


def half_starts(core, half):
    return pl.multiple_of(core * half, half), pl.multiple_of((1 - core) * half, half)


def sigma_kernel(scalars, w_ref, l_ref, r_ref, own_ref, other_ref, w3, mid, acc, lines):
    step = pl.program_id(0)
    n = acc.shape[0]

    @pl.when(step == 0)
    def _():
        pieces, count, _ = w_ref.shape
        chips = pieces // SECTORS
        for piece in range(pieces):
            start = (piece % chips * SECTORS + piece // chips) * count
            lines[start : start + count] = w_ref[piece]
        part = n // chips
        for chip in range(chips):
            for t, lanes in tiles(n):
                start = chip * SECTORS * count + t * part
                high, low = halves(lines[start : start + part])
                for third, v in enumerate((high, low, high)):
                    w3[third * n + chip * part : third * n + (chip + 1) * part, lanes] = v

    @pl.when(step < scalars[0])
    def _():
        left_form(mid, mm(l_ref[0], w3[...]))
        term = mm(mid[...], r_ref[0])

        @pl.when(step == 0)
        def _():
            acc[...] = term

        @pl.when(step > 0)
        def _():
            acc[...] += term

    @pl.when(step == pl.num_programs(0) - 1)
    def _():
        chunk = n // GROUPS
        count = chunk * n // LANES
        for ref, start in zip((own_ref, other_ref), half_starts(scalars[1], n // 2), strict=True):
            for chip in range(GROUPS // 2):
                rows = pl.ds(pl.multiple_of(start + chip * chunk, chunk), chunk)
                lines_of(ref.at[chip * count : (chip + 1) * count], acc[rows])


def partial_sigma(scalars, pieces, left3, right3):
    k, n = left3.shape[:2]
    lines = n * n // LANES

    def active(w, s):
        return (jnp.minimum(w, s[0] - 1), 0, 0)

    return pl.pallas_call(
        sigma_kernel,
        out_shape=(jax.ShapeDtypeStruct((lines // 2, LANES), F32),) * 2,
        grid_spec=pltpu.PrefetchScalarGridSpec(
            num_scalar_prefetch=1,
            grid=(k,),
            in_specs=[
                pl.BlockSpec(pieces.shape, lambda w, s: (0, 0, 0)),
                pl.BlockSpec((1, n, 3 * n), active),
                pl.BlockSpec((1, 3 * n, n), active),
            ],
            out_specs=(pl.BlockSpec((lines // 2, LANES), lambda w, s: (0, 0)),) * 2,
            scratch_shapes=[
                pltpu.VMEM((3 * n, n), BF16),
                pltpu.VMEM((n, 3 * n), BF16),
                pltpu.VMEM((n, n), F32),
                pltpu.VMEM((lines, LANES), F32),
            ],
        ),
        compiler_params=params(),
        cost_estimate=cost(12 * k * n**3, 16 * k * n * n),
        name="partial_sigma",
    )(scalars, pieces, left3, right3)


def start_polar(core, mine, other, x):
    n = x.shape[0]
    total = jnp.sum(mine[...] * mine[...]) + jnp.sum(other[...] * other[...])
    factor = lax.rsqrt(n * (total / float(n * n)) + 1e-06) / 2.2
    chunk = n // GROUPS
    count = chunk * n // LANES
    for ref, start in zip((mine, other), half_starts(core, n // 2), strict=True):
        for chip in range(GROUPS // 2):
            rows = pl.ds(pl.multiple_of(start + chip * chunk, chunk), chunk)
            for t, lanes in tiles(n):
                first = chip * count + t * chunk
                x[rows, lanes] = ref[first : first + chunk] * factor


def iterate_polar(iterations, x, a, b, r):
    n = x.shape[0]

    def iteration(_, carry):
        high, low = halves(x[...])
        side_by_side(a, high, high, low)
        side_by_side(b, high, low, high)
        stacked(r, high, low, high)
        first = mm_nt(a[...], b[0:256])
        second = mm_nt(a[256:n], b[256:512])
        third = mm_nt(a[512:n], b[512:n])
        blocks_of = (
            (0, (first[0:256], first[256:n].T)),
            (256, (first[256:512], second[0:256], second[256 : n - 256].T)),
            (512, (first[512:n], second[256 : n - 256], third)),
        )
        for start, blocks in blocks_of:
            high, low = halves(jnp.concatenate(blocks, 1))
            side_by_side(a.at[start : start + high.shape[0]], high, high, low)
        x[...] = 1.5 * x[...] - 0.5 * mm(a[...], r[...])
        return carry

    lax.fori_loop(0, iterations, iteration, 0)


def polar_scratch(n):
    return [
        pltpu.VMEM((n, n), F32),
        pltpu.VMEM((n, 3 * n), BF16),
        pltpu.VMEM((n, 3 * n), BF16),
        pltpu.VMEM((3 * n, n), BF16),
    ]


def own_start_kernel(scalars, mine_ref, other_ref, o_ref, x, a, b, r):
    start_polar(scalars[0], mine_ref, other_ref, x)
    iterate_polar(EARLY, x, a, b, r)
    o_ref[...] = x[...]


def own_start(scalars, mine, other, n):
    return pl.pallas_call(
        own_start_kernel,
        grid=(1,),
        out_shape=jax.ShapeDtypeStruct((n, n), F32),
        in_specs=[pl.BlockSpec(memory_space=pltpu.SMEM), WHOLE, WHOLE],
        out_specs=pl.BlockSpec((n, n), lambda i: (0, 0)),
        scratch_shapes=polar_scratch(n),
        compiler_params=params(),
        cost_estimate=cost(EARLY * 12 * n**3, 8 * n * n),
        name="own_start",
    )(scalars, mine, other)


def own_finish_kernel(scalars, x_ref, l_ref, columns_ref, o_ref, x, a, b, r):
    @pl.when(pl.program_id(0) == 0)
    def _():
        x[...] = x_ref[...]
        iterate_polar(POLAR - EARLY, x, a, b, r)
        updated = (x[...] * math.sqrt(x.shape[0])).T
        left_form(a, updated)
        x[...] = updated
        width = columns_ref.shape[0]
        columns_ref[...] = x[pl.ds(pl.multiple_of(scalars[1] * width, width), width)]

    right_form(r, l_ref[0])
    left_form(o_ref.at[0], mm(a[...], r[...]))


def own_finish(scalars, iterate, left):
    k, n, _ = left.shape
    return pl.pallas_call(
        own_finish_kernel,
        out_shape=(jax.ShapeDtypeStruct((n // GROUPS, n), F32), jax.ShapeDtypeStruct((k, n, 3 * n), BF16)),
        grid_spec=pltpu.PrefetchScalarGridSpec(
            num_scalar_prefetch=1,
            grid=(k,),
            in_specs=[
                pl.BlockSpec((n, n), lambda w, s: (0, 0)),
                pl.BlockSpec((1, n, n), lambda w, s: (w, 0, 0)),
            ],
            out_specs=(
                pl.BlockSpec((n // GROUPS, n), lambda w, s: (0, 0)),
                pl.BlockSpec((1, n, 3 * n), lambda w, s: (w, 0, 0)),
            ),
            scratch_shapes=polar_scratch(n),
        ),
        compiler_params=params(),
        cost_estimate=cost(((POLAR - EARLY) * 12 + 6 * k) * n**3, 10 * k * n * n),
        name="own_finish",
    )(scalars, iterate, left)


def source_kernel(scalars, p_ref, h_ref, o_ref, x, a, b, r, mine, other):
    @pl.when(pl.program_id(0) == 0)
    def _():
        pieces, count, _ = p_ref.shape
        chips, part = pieces // SECTORS, count // 2
        for piece in range(pieces):
            start = (piece % chips * SECTORS + piece // chips) * part
            mine[start : start + part] = p_ref[piece, 0:part]
            other[start : start + part] = p_ref[piece, part:count]
        start_polar(scalars[0], mine, other, x)
        iterate_polar(POLAR, x, a, b, r)
        right_form(r, x[...] * math.sqrt(x.shape[0]))

    o_ref[0] = mm(h_ref[0], r[...])


def rotate_by_source(scalars, pieces, half3):
    k, n, _ = half3.shape
    half_lines = pltpu.VMEM((n * n // LANES // 2, LANES), F32)
    return pl.pallas_call(
        source_kernel,
        out_shape=jax.ShapeDtypeStruct((k, n, n), F32),
        grid_spec=pltpu.PrefetchScalarGridSpec(
            num_scalar_prefetch=1,
            grid=(k,),
            in_specs=[
                pl.BlockSpec(pieces.shape, lambda w, s: (0, 0, 0)),
                pl.BlockSpec((1, n, 3 * n), lambda w, s: (w, 0, 0)),
            ],
            out_specs=pl.BlockSpec((1, n, n), lambda w, s: (w, 0, 0)),
            scratch_shapes=polar_scratch(n) + [half_lines, half_lines],
        ),
        compiler_params=params(),
        cost_estimate=cost((POLAR * 12 + 6 * k) * n**3, 10 * k * n * n),
        name="rotate_by_source",
    )(scalars, pieces, half3)


def cut_kernel(scalars, w_ref, o_ref, part):
    lines_of(part, w_ref)
    pieces, count, _ = o_ref.shape
    for piece in range(pieces):
        o_ref[piece] = part[piece * count : (piece + 1) * count]


def cut(chip, block, chips):
    n = block.shape[0]
    rows = n // chips
    lines = rows * n // LANES
    piece_shape = (SECTORS, lines // SECTORS, LANES)
    return pl.pallas_call(
        cut_kernel,
        out_shape=jax.ShapeDtypeStruct(piece_shape, F32),
        grid_spec=pltpu.PrefetchScalarGridSpec(
            num_scalar_prefetch=1,
            grid=(1,),
            in_specs=[pl.BlockSpec((rows, n), lambda i, s: (s[0], 0))],
            out_specs=pl.BlockSpec(piece_shape, lambda i, s: (0, 0, 0)),
            scratch_shapes=[pltpu.VMEM((lines, LANES), F32)],
        ),
        compiler_params=params(),
        cost_estimate=cost(rows * n, 8 * rows * n),
        name="cut",
    )(chip, block)


def pair_kernel(mine_ref, other_ref, o_ref):
    pieces, count, _ = o_ref.shape
    part = count // 2
    for piece in range(pieces):
        lines = slice(piece * part, (piece + 1) * part)
        o_ref[piece, 0:part] = mine_ref[lines]
        o_ref[piece, part:count] = other_ref[lines]


def pair_up(mine, other):
    lines = mine.shape[0]
    return pl.pallas_call(
        pair_kernel,
        out_shape=jax.ShapeDtypeStruct((SECTORS, 2 * lines // SECTORS, LANES), F32),
        in_specs=[WHOLE, WHOLE],
        out_specs=WHOLE,
        compiler_params=params(),
        cost_estimate=cost(lines, 16 * lines * LANES),
        name="pair_up",
    )(mine, other)


def swap_cores(block):
    return lax.ppermute(block, "core", [(0, 1), (1, 0)])


def exchange(pieces, axes):
    return lax.all_to_all(pieces, axes, split_axis=0, concat_axis=0, tiled=True)


def deliver(spread, readers):
    return exchange(jnp.take(spread, readers, axis=0, mode="clip"), ("sector", "x"))


def shards(wavefunction, left_env, right_env, shift_map, op_counts):
    chips = lax.axis_size("x")
    chip, core = lax.axis_index("x"), lax.axis_index("core")
    group_here = chip * lax.axis_size("core") + core
    n = wavefunction.shape[1]
    lines = n * n // LANES
    scalars = jnp.stack([op_counts[0, 0], core.astype(jnp.int32)])
    readers = lax.all_gather(shift_map[0], "x").T.reshape(-1)
    left3, right3 = prepare(left_env[0], right_env[0])

    spread = exchange(cut(chip.astype(jnp.int32)[None], wavefunction[0], chips), "sector")
    moved = deliver(spread, readers)

    own, other = partial_sigma(scalars, moved, left3, right3)
    pair = (own + swap_cores(other)).reshape(chips, lines // 2 // chips, LANES)
    chunk = jnp.sum(exchange(pair, "x"), axis=0)

    other_chunk = swap_cores(chunk)
    spread = exchange(pair_up(chunk, other_chunk), "sector")

    where = jnp.stack([core, group_here]).astype(jnp.int32)
    mine = lax.all_gather(chunk, "x", tiled=True)
    early, spread = lax.optimization_barrier((own_start(where, mine, swap_cores(mine), n), spread))
    source_pieces = deliver(spread, readers)
    own_rows, half3 = own_finish(where, early, left_env[0])
    half3, source_pieces = lax.optimization_barrier((half3, source_pieces))
    rotated = rotate_by_source(where, source_pieces, half3)
    return (own_rows.T[None], rotated[None])


def solution(mesh):
    sectors, groups = mesh.devices.shape
    fine = Mesh(mesh.devices.reshape(sectors, groups // 2, 2), ("sector", "x", "core"))
    ops = ("x", "core")
    return jax.shard_map(
        shards,
        mesh=fine,
        in_specs=(
            P("sector", None, None),
            P("sector", ops, None, None),
            P("sector", ops, None, None),
            P(ops, None),
            P(ops, "sector"),
        ),
        out_specs=(P("sector", None, ops), P("sector", ops, None, None)),
        check_vma=False,
    )
```

```python
import functools
import math

import jax
import jax.numpy as jnp
from jax import lax
from jax.experimental import pallas as pl
from jax.experimental.pallas import tpu as pltpu
from jax.sharding import Mesh
from jax.sharding import PartitionSpec as P

POLAR = 5
SECTORS = 16
GROUPS = 8
EARLY = 2
LANES = 128
F32, BF16 = jnp.float32, jnp.bfloat16
VMEM_LIMIT = 48 << 20
ALL_VMEM = 58 << 20
WHOLE = pl.BlockSpec(memory_space=pltpu.VMEM)


def halves(v):
    high = v.astype(BF16)
    return high, (v - high.astype(F32)).astype(BF16)


def side_by_side(ref, a, b, c):
    n = a.shape[1]
    ref[:, 0:n] = a
    ref[:, n : 2 * n] = b
    ref[:, 2 * n : 3 * n] = c


def stacked(ref, a, b, c):
    n = a.shape[0]
    ref[0:n] = a
    ref[n : 2 * n] = b
    ref[2 * n : 3 * n] = c


def left_form(ref, v):
    high, low = halves(v)
    side_by_side(ref, high, high, low)


def right_form(ref, v):
    high, low = halves(v)
    stacked(ref, high, low, high)


def mm(a, b):
    return jnp.dot(a, b, preferred_element_type=F32)


def mm_nt(a, b):
    return lax.dot_general(a, b, (((1,), (1,)), ((), ())), preferred_element_type=F32)


def params(limit=VMEM_LIMIT):
    return pltpu.CompilerParams(vmem_limit_bytes=limit)


def cost(flops, nbytes):
    return pl.CostEstimate(flops=int(flops), bytes_accessed=int(nbytes), transcendentals=0)


def prepare_kernel(l_ref, r_ref, lo_ref, ro_ref, ls_ref):
    left_form(lo_ref.at[0], l_ref[0])
    right_form(ls_ref, l_ref[0])
    right_form(ro_ref.at[0], r_ref[0])


def prepare(left, right):
    k, n, _ = left.shape
    block = pl.BlockSpec((1, n, n), lambda w: (w, 0, 0))
    return pl.pallas_call(
        prepare_kernel,
        grid=(k,),
        out_shape=(
            jax.ShapeDtypeStruct((k, n, 3 * n), BF16),
            jax.ShapeDtypeStruct((k, 3 * n, n), BF16),
            jax.ShapeDtypeStruct((3 * n, k * n), BF16),
        ),
        in_specs=[block, block],
        out_specs=(
            pl.BlockSpec((1, n, 3 * n), lambda w: (w, 0, 0)),
            pl.BlockSpec((1, 3 * n, n), lambda w: (w, 0, 0)),
            pl.BlockSpec((3 * n, n), lambda w: (0, w)),
        ),
        compiler_params=params(),
        cost_estimate=cost(12 * k * n * n, 26 * k * n * n),
        name="prepare",
    )(left, right)


def tiles(n):
    return [(t, slice(t * LANES, (t + 1) * LANES)) for t in range(n // LANES)]


def lines_of(ref, v):
    count = v.shape[0]
    for t, lanes in tiles(v.shape[1]):
        ref[t * count : (t + 1) * count] = v[:, lanes]


def half_starts(core, half):
    return pl.multiple_of(core * half, half), pl.multiple_of((1 - core) * half, half)


def sigma_kernel(scalars, w_ref, l_ref, r_ref, own_ref, other_ref, w3, mid, acc, lines):
    step = pl.program_id(0)
    n = acc.shape[0]

    @pl.when(step == 0)
    def _():
        pieces, count, _ = w_ref.shape
        chips = pieces // SECTORS
        for piece in range(pieces):
            start = (piece % chips * SECTORS + piece // chips) * count
            lines[start : start + count] = w_ref[piece]
        part = n // chips
        for chip in range(chips):
            for t, lanes in tiles(n):
                start = chip * SECTORS * count + t * part
                high, low = halves(lines[start : start + part])
                for third, v in enumerate((high, low, high)):
                    w3[third * n + chip * part : third * n + (chip + 1) * part, lanes] = v

    @pl.when(step < scalars[0])
    def _():
        left_form(mid, mm(l_ref[0], w3[...]))
        term = mm(mid[...], r_ref[0])

        @pl.when(step == 0)
        def _():
            acc[...] = term

        @pl.when(step > 0)
        def _():
            acc[...] += term

    @pl.when(step == pl.num_programs(0) - 1)
    def _():
        chunk = n // GROUPS
        count = chunk * n // LANES
        for ref, start in zip((own_ref, other_ref), half_starts(scalars[1], n // 2), strict=True):
            for chip in range(GROUPS // 2):
                rows = pl.ds(pl.multiple_of(start + chip * chunk, chunk), chunk)
                lines_of(ref.at[chip * count : (chip + 1) * count], acc[rows])


def partial_sigma(scalars, pieces, left3, right3):
    k, n = left3.shape[:2]
    lines = n * n // LANES

    def active(w, s):
        return (jnp.minimum(w, s[0] - 1), 0, 0)

    return pl.pallas_call(
        sigma_kernel,
        out_shape=(jax.ShapeDtypeStruct((lines // 2, LANES), F32),) * 2,
        grid_spec=pltpu.PrefetchScalarGridSpec(
            num_scalar_prefetch=1,
            grid=(k,),
            in_specs=[
                pl.BlockSpec(pieces.shape, lambda w, s: (0, 0, 0)),
                pl.BlockSpec((1, n, 3 * n), active),
                pl.BlockSpec((1, 3 * n, n), active),
            ],
            out_specs=(pl.BlockSpec((lines // 2, LANES), lambda w, s: (0, 0)),) * 2,
            scratch_shapes=[
                pltpu.VMEM((3 * n, n), BF16),
                pltpu.VMEM((n, 3 * n), BF16),
                pltpu.VMEM((n, n), F32),
                pltpu.VMEM((lines, LANES), F32),
            ],
        ),
        compiler_params=params(),
        cost_estimate=cost(12 * k * n**3, 16 * k * n * n),
        name="partial_sigma",
    )(scalars, pieces, left3, right3)


def start_polar(core, mine, other, x):
    n = x.shape[0]
    total = jnp.sum(mine[...] * mine[...]) + jnp.sum(other[...] * other[...])
    factor = lax.rsqrt(n * (total / float(n * n)) + 1e-06) / 2.2
    chunk = n // GROUPS
    count = chunk * n // LANES
    for ref, start in zip((mine, other), half_starts(core, n // 2), strict=True):
        for chip in range(GROUPS // 2):
            rows = pl.ds(pl.multiple_of(start + chip * chunk, chunk), chunk)
            for t, lanes in tiles(n):
                first = chip * count + t * chunk
                x[rows, lanes] = ref[first : first + chunk] * factor


def symmetric_rows(a, b):
    n = a.shape[0]
    first = mm_nt(a[...], b[0:256])
    second = mm_nt(a[256:n], b[256:512])
    third = mm_nt(a[512:n], b[512:n])
    return (
        (slice(0, 256), jnp.concatenate((first[0:256], first[256:n].T), 1)),
        (slice(256, 512), jnp.concatenate((first[256:512], second[0:256], second[256 : n - 256].T), 1)),
        (slice(512, n), jnp.concatenate((first[512:n], second[256 : n - 256], third), 1)),
    )


def split_iterate(x, a, b, r):
    high, low = halves(x[...])
    side_by_side(a, high, high, low)
    side_by_side(b, high, low, high)
    stacked(r, high, low, high)


def iterate_once(x, a, b, r):
    split_iterate(x, a, b, r)
    for rows, v in symmetric_rows(a, b):
        left_form(a.at[rows], v)
    x[...] = 1.5 * x[...] - 0.5 * mm(a[...], r[...])


def iterate_twice(x, a, b, r, g):
    split_iterate(x, a, b, r)
    for rows, v in symmetric_rows(a, b):
        g[rows] = v
    high, low = halves(g[...])
    side_by_side(a, high, high, low)
    side_by_side(b, high, low, high)
    n = x.shape[0]
    for rows, q in symmetric_rows(a, b):
        gram = g[rows]
        left_form(a.at[rows], q)
        high, low = halves(0.0625 * q - 0.5625 * gram)
        side_by_side(b.at[rows], high, low, high)
        row = lax.broadcasted_iota(jnp.int32, q.shape, 0) + rows.start
        diagonal = row == lax.broadcasted_iota(jnp.int32, q.shape, 1)
        g[rows] = 1.6875 * q - 2.4375 * gram + jnp.where(diagonal, 2.25, 0.0)
    for rows, v in symmetric_rows(a, b):
        left_form(a.at[rows], g[rows] + v)
    x[...] = mm(a[...], r[...])


def iterate_polar(iterations, x, a, b, r, g):
    def twice(_, carry):
        iterate_twice(x, a, b, r, g)
        return carry

    lax.fori_loop(0, iterations // 2, twice, 0)
    if iterations % 2:
        iterate_once(x, a, b, r)


def iterate_singly(iterations, x, a, b, r):
    def once(_, carry):
        iterate_once(x, a, b, r)
        return carry

    lax.fori_loop(0, iterations, once, 0)


def polar_scratch(n):
    return [
        pltpu.VMEM((n, n), F32),
        pltpu.VMEM((n, 3 * n), BF16),
        pltpu.VMEM((n, 3 * n), BF16),
        pltpu.VMEM((3 * n, n), BF16),
        pltpu.VMEM((n, n), F32),
    ]


def own_start_kernel(scalars, mine_ref, other_ref, o_ref, x, a, b, r, g, sem):
    start_polar(scalars[0], mine_ref, other_ref, x)
    iterate_singly(EARLY, x, a, b, r)
    copy = pltpu.make_async_copy(x, o_ref, sem)
    copy.start()
    copy.wait()


def own_start(scalars, mine, other, n):
    return pl.pallas_call(
        own_start_kernel,
        out_shape=jax.ShapeDtypeStruct((n, n), F32),
        in_specs=[pl.BlockSpec(memory_space=pltpu.SMEM), WHOLE, WHOLE],
        out_specs=pl.BlockSpec(memory_space=pltpu.HBM),
        scratch_shapes=polar_scratch(n) + [pltpu.SemaphoreType.DMA],
        compiler_params=params(ALL_VMEM),
        cost_estimate=cost(EARLY * 12 * n**3, 8 * n * n),
        name="own_start",
    )(scalars, mine, other)


def own_finish_kernel(scalars, x_ref, l_ref, columns_ref, o_ref, x, a, b, r, g, blocks, result, sems, out_sems):
    n = x.shape[0]
    steps, _, width = blocks.shape
    state = pltpu.make_async_copy(x_ref, x, sems.at[steps])
    state.start()
    reads = [
        pltpu.make_async_copy(l_ref.at[:, pl.ds(step * width, width)], blocks.at[step], sems.at[step])
        for step in range(steps)
    ]
    for read in reads:
        read.start()
    state.wait()
    iterate_singly(POLAR - EARLY, x, a, b, r)
    updated = (x[...] * math.sqrt(n)).T
    left_form(a, updated)
    x[...] = updated
    count = columns_ref.shape[0]
    columns_ref[...] = x[pl.ds(pl.multiple_of(scalars[1] * count, count), count)]
    per_step = width // n

    def write(w):
        return pltpu.make_async_copy(result.at[w], o_ref.at[w], out_sems.at[w])

    def pair(step, carry):
        columns = pl.ds(pl.multiple_of(step * width, width), width)
        pltpu.make_async_copy(l_ref.at[:, columns], blocks.at[step], sems.at[step]).wait()
        product = mm(a[...], blocks[step])
        for k in range(per_step):
            w = step * per_step + k
            left_form(result.at[w], product[:, k * n : (k + 1) * n])
            write(w).start()
        return carry

    lax.fori_loop(0, steps, pair, 0)
    for w in range(steps * per_step):
        write(w).wait()


def own_finish(scalars, iterate, stacked_left):
    n = iterate.shape[0]
    k = stacked_left.shape[1] // n
    hbm = pl.BlockSpec(memory_space=pltpu.HBM)
    return pl.pallas_call(
        own_finish_kernel,
        out_shape=(jax.ShapeDtypeStruct((n // GROUPS, n), F32), jax.ShapeDtypeStruct((k, n, 3 * n), BF16)),
        in_specs=[pl.BlockSpec(memory_space=pltpu.SMEM), hbm, hbm],
        out_specs=(WHOLE, hbm),
        scratch_shapes=polar_scratch(n)
        + [
            pltpu.VMEM((k // 2, 3 * n, 2 * n), BF16),
            pltpu.VMEM((k, n, 3 * n), BF16),
            pltpu.SemaphoreType.DMA((k // 2 + 1,)),
            pltpu.SemaphoreType.DMA((k,)),
        ],
        compiler_params=params(),
        cost_estimate=cost(((POLAR - EARLY) * 12 + 6 * k) * n**3, 14 * k * n * n),
        name="own_finish",
    )(scalars, iterate, stacked_left)


def source_kernel(scalars, p_ref, h_ref, o_ref, x, a, b, r, g, mine, other, blocks, result, sems, out_sems):
    n = x.shape[0]
    operators = blocks.shape[0]
    reads = [pltpu.make_async_copy(h_ref.at[w], blocks.at[w], sems.at[w]) for w in range(operators)]
    for read in reads:
        read.start()
    pieces, count, _ = p_ref.shape
    chips, part = pieces // SECTORS, count // 2
    for piece in range(pieces):
        start = (piece % chips * SECTORS + piece // chips) * part
        mine[start : start + part] = p_ref[piece, 0:part]
        other[start : start + part] = p_ref[piece, part:count]
    start_polar(scalars[0], mine, other, x)
    iterate_polar(POLAR, x, a, b, r, g)
    right_form(r, x[...] * math.sqrt(n))

    def write(w):
        return pltpu.make_async_copy(result.at[w], o_ref.at[w], out_sems.at[w])

    def operator(w, carry):
        pltpu.make_async_copy(h_ref.at[w], blocks.at[w], sems.at[w]).wait()
        result[w] = mm(blocks[w], r[...])
        write(w).start()
        return carry

    lax.fori_loop(0, operators, operator, 0)
    for w in range(operators):
        write(w).wait()


def rotate_by_source(scalars, pieces, half3):
    k, n, _ = half3.shape
    half_lines = pltpu.VMEM((n * n // LANES // 2, LANES), F32)
    hbm = pl.BlockSpec(memory_space=pltpu.HBM)
    return pl.pallas_call(
        source_kernel,
        out_shape=jax.ShapeDtypeStruct((k, n, n), F32),
        in_specs=[pl.BlockSpec(memory_space=pltpu.SMEM), WHOLE, hbm],
        out_specs=hbm,
        scratch_shapes=polar_scratch(n)
        + [
            half_lines,
            half_lines,
            pltpu.VMEM((k, n, 3 * n), BF16),
            pltpu.VMEM((k, n, n), F32),
            pltpu.SemaphoreType.DMA((k,)),
            pltpu.SemaphoreType.DMA((k,)),
        ],
        compiler_params=params(),
        cost_estimate=cost((POLAR * 12 + 6 * k) * n**3, 10 * k * n * n),
        name="rotate_by_source",
    )(scalars, pieces, half3)


def cut_kernel(chip_ref, w_ref, o_ref, block, part, sem):
    rows = block.shape[0]
    here = pl.ds(pl.multiple_of(chip_ref[0] * rows, rows), rows)
    copy = pltpu.make_async_copy(w_ref.at[here], block, sem)
    copy.start()
    copy.wait()
    lines_of(part, block)
    pieces, count, _ = o_ref.shape
    for piece in range(pieces):
        o_ref[piece] = part[piece * count : (piece + 1) * count]


def cut(chip, block, chips):
    n = block.shape[0]
    rows = n // chips
    lines = rows * n // LANES
    return pl.pallas_call(
        cut_kernel,
        out_shape=jax.ShapeDtypeStruct((SECTORS, lines // SECTORS, LANES), F32),
        in_specs=[pl.BlockSpec(memory_space=pltpu.SMEM), pl.BlockSpec(memory_space=pltpu.HBM)],
        out_specs=WHOLE,
        scratch_shapes=[pltpu.VMEM((rows, n), F32), pltpu.VMEM((lines, LANES), F32), pltpu.SemaphoreType.DMA],
        compiler_params=params(ALL_VMEM),
        cost_estimate=cost(rows * n, 8 * rows * n),
        name="cut",
    )(chip, block)


def pair_kernel(mine_ref, other_ref, o_ref):
    pieces, count, _ = o_ref.shape
    part = count // 2
    for piece in range(pieces):
        lines = slice(piece * part, (piece + 1) * part)
        o_ref[piece, 0:part] = mine_ref[lines]
        o_ref[piece, part:count] = other_ref[lines]


def pair_up(mine, other):
    lines = mine.shape[0]
    return pl.pallas_call(
        pair_kernel,
        out_shape=jax.ShapeDtypeStruct((SECTORS, 2 * lines // SECTORS, LANES), F32),
        in_specs=[WHOLE, WHOLE],
        out_specs=WHOLE,
        compiler_params=params(),
        cost_estimate=cost(lines, 16 * lines * LANES),
        name="pair_up",
    )(mine, other)


def swap_cores(block):
    return lax.ppermute(block, "core", [(0, 1), (1, 0)])


def exchange(pieces, axes):
    return lax.all_to_all(pieces, axes, split_axis=0, concat_axis=0, tiled=True)


def deliver(spread, readers):
    return exchange(jnp.take(spread, readers, axis=0, mode="clip"), ("sector", "x"))


def shards(wavefunction, left_env, right_env, shift_map, op_counts):
    chips = lax.axis_size("x")
    chip, core = lax.axis_index("x"), lax.axis_index("core")
    group_here = chip * lax.axis_size("core") + core
    n = wavefunction.shape[1]
    lines = n * n // LANES
    scalars = jnp.stack([op_counts[0, 0], core.astype(jnp.int32)])
    readers = lax.all_gather(shift_map[0], "x").T.reshape(-1)
    left3, right3, stacked_left = prepare(left_env[0], right_env[0])

    spread = exchange(cut(chip.astype(jnp.int32)[None], wavefunction[0], chips), "sector")
    moved = deliver(spread, readers)

    own, other = partial_sigma(scalars, moved, left3, right3)
    pair = (own + swap_cores(other)).reshape(chips, lines // 2 // chips, LANES)
    chunk = jnp.sum(exchange(pair, "x"), axis=0)

    other_chunk = swap_cores(chunk)
    spread = exchange(pair_up(chunk, other_chunk), "sector")

    where = jnp.stack([core, group_here]).astype(jnp.int32)
    mine = lax.all_gather(chunk, "x", tiled=True)
    early, spread = lax.optimization_barrier((own_start(where, mine, swap_cores(mine), n), spread))
    source_pieces = deliver(spread, readers)
    own_rows, half3 = own_finish(where, early, stacked_left)
    half3, source_pieces = lax.optimization_barrier((half3, source_pieces))
    rotated = rotate_by_source(where, source_pieces, half3)
    return (own_rows.T[None], rotated[None])


def solution(mesh):
    sectors, groups = mesh.devices.shape
    fine = Mesh(mesh.devices.reshape(sectors, groups // 2, 2), ("sector", "x", "core"))
    ops = ("x", "core")
    return jax.shard_map(
        shards,
        mesh=fine,
        in_specs=(
            P("sector", None, None),
            P("sector", ops, None, None),
            P("sector", ops, None, None),
            P(ops, None),
            P(ops, "sector"),
        ),
        out_specs=(P("sector", None, ops), P("sector", ops, None, None)),
        check_vma=False,
    )
```

```python
import functools
import math

import jax
import jax.numpy as jnp
from jax import lax
from jax.experimental import pallas as pl
from jax.experimental.pallas import tpu as pltpu
from jax.sharding import Mesh
from jax.sharding import PartitionSpec as P

POLAR = 5
SECTORS = 16
GROUPS = 8
EARLY = 1
LANES = 128
F32, BF16 = jnp.float32, jnp.bfloat16
VMEM_LIMIT = 48 << 20
ALL_VMEM = 58 << 20
WHOLE = pl.BlockSpec(memory_space=pltpu.VMEM)


def halves(v):
    high = v.astype(BF16)
    return high, (v - high.astype(F32)).astype(BF16)


def side_by_side(ref, a, b, c):
    n = a.shape[1]
    ref[:, 0:n] = a
    ref[:, n : 2 * n] = b
    ref[:, 2 * n : 3 * n] = c


def stacked(ref, a, b, c):
    n = a.shape[0]
    ref[0:n] = a
    ref[n : 2 * n] = b
    ref[2 * n : 3 * n] = c


def left_form(ref, v):
    high, low = halves(v)
    side_by_side(ref, high, high, low)


def right_form(ref, v):
    high, low = halves(v)
    stacked(ref, high, low, high)


def mm(a, b):
    return jnp.dot(a, b, preferred_element_type=F32)


def mm_nt(a, b):
    return lax.dot_general(a, b, (((1,), (1,)), ((), ())), preferred_element_type=F32)


def params(limit=VMEM_LIMIT):
    return pltpu.CompilerParams(vmem_limit_bytes=limit)


def cost(flops, nbytes):
    return pl.CostEstimate(flops=int(flops), bytes_accessed=int(nbytes), transcendentals=0)


def prepare_kernel(l_ref, r_ref, lo_ref, ro_ref, ls_ref):
    left_form(lo_ref.at[0], l_ref[0])
    right_form(ls_ref, l_ref[0])
    right_form(ro_ref.at[0], r_ref[0])


def prepare(left, right):
    k, n, _ = left.shape
    block = pl.BlockSpec((1, n, n), lambda w: (w, 0, 0))
    return pl.pallas_call(
        prepare_kernel,
        grid=(k,),
        out_shape=(
            jax.ShapeDtypeStruct((k, n, 3 * n), BF16),
            jax.ShapeDtypeStruct((k, 3 * n, n), BF16),
            jax.ShapeDtypeStruct((3 * n, k * n), BF16),
        ),
        in_specs=[block, block],
        out_specs=(
            pl.BlockSpec((1, n, 3 * n), lambda w: (w, 0, 0)),
            pl.BlockSpec((1, 3 * n, n), lambda w: (w, 0, 0)),
            pl.BlockSpec((3 * n, n), lambda w: (0, w)),
        ),
        compiler_params=params(),
        cost_estimate=cost(12 * k * n * n, 26 * k * n * n),
        name="prepare",
    )(left, right)


def tiles(n):
    return [(t, slice(t * LANES, (t + 1) * LANES)) for t in range(n // LANES)]


def lines_of(ref, v):
    count = v.shape[0]
    for t, lanes in tiles(v.shape[1]):
        ref[t * count : (t + 1) * count] = v[:, lanes]


def half_starts(core, half):
    return pl.multiple_of(core * half, half), pl.multiple_of((1 - core) * half, half)


def sigma_kernel(scalars, w_ref, l_ref, r_ref, own_ref, other_ref, w3, mid, acc, lines):
    step = pl.program_id(0)
    n = acc.shape[0]

    @pl.when(step == 0)
    def _():
        pieces, count, _ = w_ref.shape
        chips = pieces // SECTORS
        for piece in range(pieces):
            start = (piece % chips * SECTORS + piece // chips) * count
            lines[start : start + count] = w_ref[piece]
        part = n // chips
        for chip in range(chips):
            for t, lanes in tiles(n):
                start = chip * SECTORS * count + t * part
                high, low = halves(lines[start : start + part])
                for third, v in enumerate((high, low, high)):
                    w3[third * n + chip * part : third * n + (chip + 1) * part, lanes] = v

    @pl.when(step < scalars[0])
    def _():
        left_form(mid, mm(l_ref[0], w3[...]))
        term = mm(mid[...], r_ref[0])

        @pl.when(step == 0)
        def _():
            acc[...] = term

        @pl.when(step > 0)
        def _():
            acc[...] += term

    @pl.when(step == pl.num_programs(0) - 1)
    def _():
        chunk = n // GROUPS
        count = chunk * n // LANES
        for ref, start in zip((own_ref, other_ref), half_starts(scalars[1], n // 2), strict=True):
            for chip in range(GROUPS // 2):
                rows = pl.ds(pl.multiple_of(start + chip * chunk, chunk), chunk)
                lines_of(ref.at[chip * count : (chip + 1) * count], acc[rows])


def partial_sigma(scalars, pieces, left3, right3):
    k, n = left3.shape[:2]
    lines = n * n // LANES

    def active(w, s):
        return (jnp.minimum(w, s[0] - 1), 0, 0)

    return pl.pallas_call(
        sigma_kernel,
        out_shape=(jax.ShapeDtypeStruct((lines // 2, LANES), F32),) * 2,
        grid_spec=pltpu.PrefetchScalarGridSpec(
            num_scalar_prefetch=1,
            grid=(k,),
            in_specs=[
                pl.BlockSpec(pieces.shape, lambda w, s: (0, 0, 0)),
                pl.BlockSpec((1, n, 3 * n), active),
                pl.BlockSpec((1, 3 * n, n), active),
            ],
            out_specs=(pl.BlockSpec((lines // 2, LANES), lambda w, s: (0, 0)),) * 2,
            scratch_shapes=[
                pltpu.VMEM((3 * n, n), BF16),
                pltpu.VMEM((n, 3 * n), BF16),
                pltpu.VMEM((n, n), F32),
                pltpu.VMEM((lines, LANES), F32),
            ],
        ),
        compiler_params=params(),
        cost_estimate=cost(12 * k * n**3, 16 * k * n * n),
        name="partial_sigma",
    )(scalars, pieces, left3, right3)


def start_polar(parts, x):
    n = x.shape[0]
    total = sum(jnp.sum(lines[...] * lines[...]) for lines, _ in parts)
    factor = lax.rsqrt(n * (total / float(n * n)) + 1e-06) / 2.2
    for lines, start in parts:
        count = lines.shape[0] * LANES // n
        rows = pl.ds(pl.multiple_of(start, count), count)
        for t, lanes in tiles(n):
            x[rows, lanes] = lines[t * count : (t + 1) * count] * factor


def symmetric_rows(a, b):
    n = a.shape[0]
    first = mm_nt(a[...], b[0:256])
    second = mm_nt(a[256:n], b[256:512])
    third = mm_nt(a[512:n], b[512:n])
    return (
        (slice(0, 256), jnp.concatenate((first[0:256], first[256:n].T), 1)),
        (slice(256, 512), jnp.concatenate((first[256:512], second[0:256], second[256 : n - 256].T), 1)),
        (slice(512, n), jnp.concatenate((first[512:n], second[256 : n - 256], third), 1)),
    )


def split_iterate(x, a, b, r):
    high, low = halves(x[...])
    side_by_side(a, high, high, low)
    side_by_side(b, high, low, high)
    stacked(r, high, low, high)


def iterate_once(x, a, b, r):
    split_iterate(x, a, b, r)
    for rows, v in symmetric_rows(a, b):
        left_form(a.at[rows], v)
    x[...] = 1.5 * x[...] - 0.5 * mm(a[...], r[...])


def iterate_twice(x, a, b, r, g):
    split_iterate(x, a, b, r)
    for rows, v in symmetric_rows(a, b):
        g[rows] = v
    high, low = halves(g[...])
    side_by_side(a, high, high, low)
    side_by_side(b, high, low, high)
    n = x.shape[0]
    for rows, q in symmetric_rows(a, b):
        gram = g[rows]
        left_form(a.at[rows], q)
        high, low = halves(0.0625 * q - 0.5625 * gram)
        side_by_side(b.at[rows], high, low, high)
        row = lax.broadcasted_iota(jnp.int32, q.shape, 0) + rows.start
        diagonal = row == lax.broadcasted_iota(jnp.int32, q.shape, 1)
        g[rows] = 1.6875 * q - 2.4375 * gram + jnp.where(diagonal, 2.25, 0.0)
    for rows, v in symmetric_rows(a, b):
        left_form(a.at[rows], g[rows] + v)
    x[...] = mm(a[...], r[...])


def iterate_polar(iterations, x, a, b, r, g):
    def twice(_, carry):
        iterate_twice(x, a, b, r, g)
        return carry

    lax.fori_loop(0, iterations // 2, twice, 0)
    if iterations % 2:
        iterate_once(x, a, b, r)


def iterate_singly(iterations, x, a, b, r):
    def once(_, carry):
        iterate_once(x, a, b, r)
        return carry

    lax.fori_loop(0, iterations, once, 0)


def polar_scratch(n):
    return [
        pltpu.VMEM((n, n), F32),
        pltpu.VMEM((n, 3 * n), BF16),
        pltpu.VMEM((n, 3 * n), BF16),
        pltpu.VMEM((3 * n, n), BF16),
        pltpu.VMEM((n, n), F32),
    ]


def own_start_kernel(scalars, *refs):
    gathered, (o_ref, x, a, b, r, _, sem) = refs[:GROUPS], refs[GROUPS:]
    n = x.shape[0]
    chips = GROUPS // 2
    parts = []
    for core, first in enumerate(half_starts(scalars[0], n // 2)):
        for ahead in range(chips):
            start = first + lax.rem(scalars[2] + ahead, chips) * (n // GROUPS)
            parts.append((gathered[core * chips + ahead], start))
    start_polar(parts, x)
    iterate_singly(EARLY, x, a, b, r)
    copy = pltpu.make_async_copy(x, o_ref, sem)
    copy.start()
    copy.wait()


def own_start(scalars, gathered, n):
    return pl.pallas_call(
        own_start_kernel,
        out_shape=jax.ShapeDtypeStruct((n, n), F32),
        in_specs=[pl.BlockSpec(memory_space=pltpu.SMEM)] + [WHOLE] * GROUPS,
        out_specs=pl.BlockSpec(memory_space=pltpu.HBM),
        scratch_shapes=polar_scratch(n) + [pltpu.SemaphoreType.DMA],
        compiler_params=params(ALL_VMEM),
        cost_estimate=cost(EARLY * 12 * n**3, 8 * n * n),
        name="own_start",
    )(scalars, *gathered)


def own_finish_kernel(scalars, x_ref, l_ref, columns_ref, o_ref, x, a, b, r, g, blocks, result, sems, out_sems):
    n = x.shape[0]
    steps, _, width = blocks.shape
    state = pltpu.make_async_copy(x_ref, x, sems.at[steps])
    state.start()
    reads = [
        pltpu.make_async_copy(l_ref.at[:, pl.ds(step * width, width)], blocks.at[step], sems.at[step])
        for step in range(steps)
    ]
    for read in reads:
        read.start()
    state.wait()
    iterate_singly(POLAR - EARLY, x, a, b, r)
    updated = (x[...] * math.sqrt(n)).T
    left_form(a, updated)
    x[...] = updated
    count = columns_ref.shape[0]
    columns_ref[...] = x[pl.ds(pl.multiple_of(scalars[1] * count, count), count)]
    per_step = width // n

    def write(w):
        return pltpu.make_async_copy(result.at[w], o_ref.at[w], out_sems.at[w])

    def pair(step, carry):
        columns = pl.ds(pl.multiple_of(step * width, width), width)
        pltpu.make_async_copy(l_ref.at[:, columns], blocks.at[step], sems.at[step]).wait()
        product = mm(a[...], blocks[step])
        for k in range(per_step):
            w = step * per_step + k
            left_form(result.at[w], product[:, k * n : (k + 1) * n])
            write(w).start()
        return carry

    lax.fori_loop(0, steps, pair, 0)
    for w in range(steps * per_step):
        write(w).wait()


def own_finish(scalars, iterate, stacked_left):
    n = iterate.shape[0]
    k = stacked_left.shape[1] // n
    hbm = pl.BlockSpec(memory_space=pltpu.HBM)
    return pl.pallas_call(
        own_finish_kernel,
        out_shape=(jax.ShapeDtypeStruct((n // GROUPS, n), F32), jax.ShapeDtypeStruct((k, n, 3 * n), BF16)),
        in_specs=[pl.BlockSpec(memory_space=pltpu.SMEM), hbm, hbm],
        out_specs=(WHOLE, hbm),
        scratch_shapes=polar_scratch(n)
        + [
            pltpu.VMEM((k // 2, 3 * n, 2 * n), BF16),
            pltpu.VMEM((k, n, 3 * n), BF16),
            pltpu.SemaphoreType.DMA((k // 2 + 1,)),
            pltpu.SemaphoreType.DMA((k,)),
        ],
        compiler_params=params(),
        cost_estimate=cost(((POLAR - EARLY) * 12 + 6 * k) * n**3, 14 * k * n * n),
        name="own_finish",
    )(scalars, iterate, stacked_left)


def source_kernel(scalars, p_ref, h_ref, o_ref, x, a, b, r, g, mine, other, blocks, result, sems, out_sems):
    n = x.shape[0]
    operators = blocks.shape[0]
    reads = [pltpu.make_async_copy(h_ref.at[w], blocks.at[w], sems.at[w]) for w in range(operators)]
    for read in reads:
        read.start()
    pieces, count, _ = p_ref.shape
    chips, part = pieces // SECTORS, count // 2
    for piece in range(pieces):
        start = (piece % chips * SECTORS + piece // chips) * part
        mine[start : start + part] = p_ref[piece, 0:part]
        other[start : start + part] = p_ref[piece, part:count]
    lines, rows = mine.shape[0] // chips, n // GROUPS
    parts = []
    for ref, first in zip((mine, other), half_starts(scalars[0], n // 2), strict=True):
        for chip in range(chips):
            parts.append((ref.at[chip * lines : (chip + 1) * lines], first + chip * rows))
    start_polar(parts, x)
    iterate_polar(POLAR, x, a, b, r, g)
    right_form(r, x[...] * math.sqrt(n))

    def write(w):
        return pltpu.make_async_copy(result.at[w], o_ref.at[w], out_sems.at[w])

    def operator(w, carry):
        pltpu.make_async_copy(h_ref.at[w], blocks.at[w], sems.at[w]).wait()
        result[w] = mm(blocks[w], r[...])
        write(w).start()
        return carry

    lax.fori_loop(0, operators, operator, 0)
    for w in range(operators):
        write(w).wait()


def rotate_by_source(scalars, pieces, half3):
    k, n, _ = half3.shape
    half_lines = pltpu.VMEM((n * n // LANES // 2, LANES), F32)
    hbm = pl.BlockSpec(memory_space=pltpu.HBM)
    return pl.pallas_call(
        source_kernel,
        out_shape=jax.ShapeDtypeStruct((k, n, n), F32),
        in_specs=[pl.BlockSpec(memory_space=pltpu.SMEM), WHOLE, hbm],
        out_specs=hbm,
        scratch_shapes=polar_scratch(n)
        + [
            half_lines,
            half_lines,
            pltpu.VMEM((k, n, 3 * n), BF16),
            pltpu.VMEM((k, n, n), F32),
            pltpu.SemaphoreType.DMA((k,)),
            pltpu.SemaphoreType.DMA((k,)),
        ],
        compiler_params=params(),
        cost_estimate=cost((POLAR * 12 + 6 * k) * n**3, 10 * k * n * n),
        name="rotate_by_source",
    )(scalars, pieces, half3)


def cut_kernel(chip_ref, w_ref, o_ref, block, part, sem):
    rows = block.shape[0]
    here = pl.ds(pl.multiple_of(chip_ref[0] * rows, rows), rows)
    copy = pltpu.make_async_copy(w_ref.at[here], block, sem)
    copy.start()
    copy.wait()
    lines_of(part, block)
    pieces, count, _ = o_ref.shape
    for piece in range(pieces):
        o_ref[piece] = part[piece * count : (piece + 1) * count]


def cut(chip, block, chips):
    n = block.shape[0]
    rows = n // chips
    lines = rows * n // LANES
    return pl.pallas_call(
        cut_kernel,
        out_shape=jax.ShapeDtypeStruct((SECTORS, lines // SECTORS, LANES), F32),
        in_specs=[pl.BlockSpec(memory_space=pltpu.SMEM), pl.BlockSpec(memory_space=pltpu.HBM)],
        out_specs=WHOLE,
        scratch_shapes=[pltpu.VMEM((rows, n), F32), pltpu.VMEM((lines, LANES), F32), pltpu.SemaphoreType.DMA],
        compiler_params=params(ALL_VMEM),
        cost_estimate=cost(rows * n, 8 * rows * n),
        name="cut",
    )(chip, block)


def pair_kernel(mine_ref, other_ref, o_ref):
    pieces, count, _ = o_ref.shape
    part = count // 2
    for piece in range(pieces):
        lines = slice(piece * part, (piece + 1) * part)
        o_ref[piece, 0:part] = mine_ref[lines]
        o_ref[piece, part:count] = other_ref[lines]


def pair_up(mine, other):
    lines = mine.shape[0]
    return pl.pallas_call(
        pair_kernel,
        out_shape=jax.ShapeDtypeStruct((SECTORS, 2 * lines // SECTORS, LANES), F32),
        in_specs=[WHOLE, WHOLE],
        out_specs=WHOLE,
        compiler_params=params(),
        cost_estimate=cost(lines, 16 * lines * LANES),
        name="pair_up",
    )(mine, other)


def from_chips(block):
    chips = lax.axis_size("x")
    return [block] + [
        lax.ppermute(block, "x", [(j, (j - ahead) % chips) for j in range(chips)]) for ahead in range(1, chips)
    ]


def swap_cores(block):
    return lax.ppermute(block, "core", [(0, 1), (1, 0)])


def exchange(pieces, axes):
    return lax.all_to_all(pieces, axes, split_axis=0, concat_axis=0, tiled=True)


def deliver(spread, readers):
    return exchange(jnp.take(spread, readers, axis=0, mode="clip"), ("sector", "x"))


def shards(wavefunction, left_env, right_env, shift_map, op_counts):
    chips = lax.axis_size("x")
    chip, core = lax.axis_index("x"), lax.axis_index("core")
    group_here = chip * lax.axis_size("core") + core
    n = wavefunction.shape[1]
    lines = n * n // LANES
    scalars = jnp.stack([op_counts[0, 0], core.astype(jnp.int32)])
    readers = lax.all_gather(shift_map[0], "x").T.reshape(-1)
    left3, right3, stacked_left = prepare(left_env[0], right_env[0])

    spread = exchange(cut(chip.astype(jnp.int32)[None], wavefunction[0], chips), "sector")
    moved = deliver(spread, readers)

    own, other = partial_sigma(scalars, moved, left3, right3)
    pair = (own + swap_cores(other)).reshape(chips, lines // 2 // chips, LANES)
    chunk = jnp.sum(exchange(pair, "x"), axis=0)

    other_chunk = swap_cores(chunk)
    spread = exchange(pair_up(chunk, other_chunk), "sector")

    where = jnp.stack([core, group_here, chip]).astype(jnp.int32)
    gathered = from_chips(chunk) + from_chips(other_chunk)
    early, spread = lax.optimization_barrier((own_start(where, gathered, n), spread))
    source_pieces = deliver(spread, readers)
    own_rows, half3 = own_finish(where, early, stacked_left)
    half3, source_pieces = lax.optimization_barrier((half3, source_pieces))
    rotated = rotate_by_source(where, source_pieces, half3)
    return (own_rows.T[None], rotated[None])


def solution(mesh):
    sectors, groups = mesh.devices.shape
    fine = Mesh(mesh.devices.reshape(sectors, groups // 2, 2), ("sector", "x", "core"))
    ops = ("x", "core")
    return jax.shard_map(
        shards,
        mesh=fine,
        in_specs=(
            P("sector", None, None),
            P("sector", ops, None, None),
            P("sector", ops, None, None),
            P(ops, None),
            P(ops, "sector"),
        ),
        out_specs=(P("sector", None, ops), P("sector", ops, None, None)),
        check_vma=False,
    )
```

```python
import functools
import math

import jax
import jax.numpy as jnp
from jax import lax
from jax.experimental import pallas as pl
from jax.experimental.pallas import tpu as pltpu
from jax.sharding import Mesh
from jax.sharding import PartitionSpec as P

POLAR = 5
SECTORS = 16
GROUPS = 8
EARLY = 1
LANES = 128
F32, BF16 = jnp.float32, jnp.bfloat16
VMEM_LIMIT = 48 << 20
ALL_VMEM = 58 << 20
WHOLE = pl.BlockSpec(memory_space=pltpu.VMEM)


def halves(v):
    high = v.astype(BF16)
    return high, (v - high.astype(F32)).astype(BF16)


def side_by_side(ref, a, b, c):
    n = a.shape[1]
    ref[:, 0:n] = a
    ref[:, n : 2 * n] = b
    ref[:, 2 * n : 3 * n] = c


def stacked(ref, a, b, c):
    n = a.shape[0]
    ref[0:n] = a
    ref[n : 2 * n] = b
    ref[2 * n : 3 * n] = c


def left_form(ref, v):
    high, low = halves(v)
    side_by_side(ref, high, high, low)


def right_form(ref, v):
    high, low = halves(v)
    stacked(ref, high, low, high)


def mm(a, b):
    return jnp.dot(a, b, preferred_element_type=F32)


def mm_nt(a, b):
    return lax.dot_general(a, b, (((1,), (1,)), ((), ())), preferred_element_type=F32)


def params(limit=VMEM_LIMIT):
    return pltpu.CompilerParams(vmem_limit_bytes=limit)


def cost(flops, nbytes):
    return pl.CostEstimate(flops=int(flops), bytes_accessed=int(nbytes), transcendentals=0)


def prepare_kernel(l_ref, r_ref, lo_ref, ro_ref, ls_ref):
    left_form(lo_ref.at[0], l_ref[0])
    right_form(ls_ref, l_ref[0])
    right_form(ro_ref.at[0], r_ref[0])


def prepare(left, right):
    k, n, _ = left.shape
    block = pl.BlockSpec((1, n, n), lambda w: (w, 0, 0))
    return pl.pallas_call(
        prepare_kernel,
        grid=(k,),
        out_shape=(
            jax.ShapeDtypeStruct((k, n, 3 * n), BF16),
            jax.ShapeDtypeStruct((k, 3 * n, n), BF16),
            jax.ShapeDtypeStruct((3 * n, k * n), BF16),
        ),
        in_specs=[block, block],
        out_specs=(
            pl.BlockSpec((1, n, 3 * n), lambda w: (w, 0, 0)),
            pl.BlockSpec((1, 3 * n, n), lambda w: (w, 0, 0)),
            pl.BlockSpec((3 * n, n), lambda w: (0, w)),
        ),
        compiler_params=params(),
        cost_estimate=cost(12 * k * n * n, 26 * k * n * n),
        name="prepare",
    )(left, right)


def tiles(n):
    return [(t, slice(t * LANES, (t + 1) * LANES)) for t in range(n // LANES)]


def lines_of(ref, v):
    count = v.shape[0]
    for t, lanes in tiles(v.shape[1]):
        ref[t * count : (t + 1) * count] = v[:, lanes]


def half_starts(core, half):
    return pl.multiple_of(core * half, half), pl.multiple_of((1 - core) * half, half)


def sigma_kernel(scalars, w_ref, l_ref, r_ref, own_ref, other_ref, w3, mid, acc, lines):
    step = pl.program_id(0)
    n = acc.shape[0]

    @pl.when(step == 0)
    def _():
        pieces, count, _ = w_ref.shape
        chips = pieces // SECTORS
        for piece in range(pieces):
            start = (piece % chips * SECTORS + piece // chips) * count
            lines[start : start + count] = w_ref[piece]
        part = n // chips
        for chip in range(chips):
            for t, lanes in tiles(n):
                start = chip * SECTORS * count + t * part
                high, low = halves(lines[start : start + part])
                for third, v in enumerate((high, low, high)):
                    w3[third * n + chip * part : third * n + (chip + 1) * part, lanes] = v

    @pl.when(step < scalars[0])
    def _():
        left_form(mid, mm(l_ref[0], w3[...]))
        term = mm(mid[...], r_ref[0])

        @pl.when(step == 0)
        def _():
            acc[...] = term

        @pl.when(step > 0)
        def _():
            acc[...] += term

    @pl.when(step == pl.num_programs(0) - 1)
    def _():
        chunk = n // GROUPS
        count = chunk * n // LANES
        for ref, start in zip((own_ref, other_ref), half_starts(scalars[1], n // 2), strict=True):
            for chip in range(GROUPS // 2):
                rows = pl.ds(pl.multiple_of(start + chip * chunk, chunk), chunk)
                lines_of(ref.at[chip * count : (chip + 1) * count], acc[rows])


def partial_sigma(scalars, pieces, left3, right3):
    k, n = left3.shape[:2]
    lines = n * n // LANES

    def active(w, s):
        return (jnp.minimum(w, s[0] - 1), 0, 0)

    return pl.pallas_call(
        sigma_kernel,
        out_shape=(jax.ShapeDtypeStruct((lines // 2, LANES), F32),) * 2,
        grid_spec=pltpu.PrefetchScalarGridSpec(
            num_scalar_prefetch=1,
            grid=(k,),
            in_specs=[
                pl.BlockSpec(pieces.shape, lambda w, s: (0, 0, 0)),
                pl.BlockSpec((1, n, 3 * n), active),
                pl.BlockSpec((1, 3 * n, n), active),
            ],
            out_specs=(pl.BlockSpec((lines // 2, LANES), lambda w, s: (0, 0)),) * 2,
            scratch_shapes=[
                pltpu.VMEM((3 * n, n), BF16),
                pltpu.VMEM((n, 3 * n), BF16),
                pltpu.VMEM((n, n), F32),
                pltpu.VMEM((lines, LANES), F32),
            ],
        ),
        compiler_params=params(),
        cost_estimate=cost(12 * k * n**3, 16 * k * n * n),
        name="partial_sigma",
    )(scalars, pieces, left3, right3)


def start_polar(parts, x):
    n = x.shape[0]
    total = sum(jnp.sum(lines[...] * lines[...]) for lines, _ in parts)
    factor = lax.rsqrt(n * (total / float(n * n)) + 1e-06) / 2.2
    for lines, start in parts:
        count = lines.shape[0] * LANES // n
        rows = pl.ds(pl.multiple_of(start, count), count)
        for t, lanes in tiles(n):
            x[rows, lanes] = lines[t * count : (t + 1) * count] * factor


def symmetric_rows(a, b):
    n = a.shape[0]
    first = mm_nt(a[...], b[0:256])
    second = mm_nt(a[256:n], b[256:512])
    third = mm_nt(a[512:n], b[512:n])
    return (
        (slice(0, 256), jnp.concatenate((first[0:256], first[256:n].T), 1)),
        (slice(256, 512), jnp.concatenate((first[256:512], second[0:256], second[256 : n - 256].T), 1)),
        (slice(512, n), jnp.concatenate((first[512:n], second[256 : n - 256], third), 1)),
    )


def split_iterate(x, a, b, r):
    high, low = halves(x[...])
    side_by_side(a, high, high, low)
    side_by_side(b, high, low, high)
    stacked(r, high, low, high)


def iterate_once(x, a, b, r):
    split_iterate(x, a, b, r)
    for rows, v in symmetric_rows(a, b):
        left_form(a.at[rows], v)
    x[...] = 1.5 * x[...] - 0.5 * mm(a[...], r[...])


def iterate_twice(x, a, b, r, g):
    split_iterate(x, a, b, r)
    for rows, v in symmetric_rows(a, b):
        g[rows] = v
    high, low = halves(g[...])
    side_by_side(a, high, high, low)
    side_by_side(b, high, low, high)
    n = x.shape[0]
    for rows, q in symmetric_rows(a, b):
        gram = g[rows]
        left_form(a.at[rows], q)
        high, low = halves(0.0625 * q - 0.5625 * gram)
        side_by_side(b.at[rows], high, low, high)
        row = lax.broadcasted_iota(jnp.int32, q.shape, 0) + rows.start
        diagonal = row == lax.broadcasted_iota(jnp.int32, q.shape, 1)
        g[rows] = 1.6875 * q - 2.4375 * gram + jnp.where(diagonal, 2.25, 0.0)
    for rows, v in symmetric_rows(a, b):
        left_form(a.at[rows], g[rows] + v)
    x[...] = mm(a[...], r[...])


def iterate_polar(iterations, x, a, b, r, g):
    def twice(_, carry):
        iterate_twice(x, a, b, r, g)
        return carry

    lax.fori_loop(0, iterations // 2, twice, 0)
    if iterations % 2:
        iterate_once(x, a, b, r)


def iterate_singly(iterations, x, a, b, r):
    def once(_, carry):
        iterate_once(x, a, b, r)
        return carry

    lax.fori_loop(0, iterations, once, 0)


def polar_scratch(n):
    return [
        pltpu.VMEM((n, n), F32),
        pltpu.VMEM((n, 3 * n), BF16),
        pltpu.VMEM((n, 3 * n), BF16),
        pltpu.VMEM((3 * n, n), BF16),
        pltpu.VMEM((n, n), F32),
    ]


def join_kernel(_, *refs):
    o_ref = refs[-1]
    lines = refs[0].shape[0]
    for k, ref in enumerate(refs[:-1]):
        o_ref[k * lines : (k + 1) * lines] = ref[...]


def join(after, blocks):
    lines, lanes = blocks[0].shape
    return pl.pallas_call(
        join_kernel,
        out_shape=jax.ShapeDtypeStruct((len(blocks) * lines, lanes), F32),
        in_specs=[pl.BlockSpec(memory_space=pltpu.HBM)] + [WHOLE] * len(blocks),
        out_specs=WHOLE,
        compiler_params=params(),
        cost_estimate=cost(lines, 8 * len(blocks) * lines * lanes),
        name="join",
    )(after, *blocks)


def own_start_kernel(scalars, mine_ref, other_ref, o_ref, x, a, b, r, _, sem):
    n = x.shape[0]
    chips = GROUPS // 2
    lines = mine_ref.shape[0] // chips
    parts = []
    for ref, first in zip((mine_ref, other_ref), half_starts(scalars[0], n // 2), strict=True):
        for ahead in range(chips):
            start = first + lax.rem(scalars[2] + ahead, chips) * (n // GROUPS)
            parts.append((ref.at[ahead * lines : (ahead + 1) * lines], start))
    start_polar(parts, x)
    iterate_singly(EARLY, x, a, b, r)
    copy = pltpu.make_async_copy(x, o_ref, sem)
    copy.start()
    copy.wait()


def own_start(scalars, mine, other, n):
    return pl.pallas_call(
        own_start_kernel,
        out_shape=jax.ShapeDtypeStruct((n, n), F32),
        in_specs=[pl.BlockSpec(memory_space=pltpu.SMEM), WHOLE, WHOLE],
        out_specs=pl.BlockSpec(memory_space=pltpu.HBM),
        scratch_shapes=polar_scratch(n) + [pltpu.SemaphoreType.DMA],
        compiler_params=params(ALL_VMEM),
        cost_estimate=cost(EARLY * 12 * n**3, 8 * n * n),
        name="own_start",
    )(scalars, mine, other)


def own_finish_kernel(scalars, x_ref, l_ref, columns_ref, o_ref, x, a, b, r, g, blocks, result, sems, out_sems):
    n = x.shape[0]
    steps, _, width = blocks.shape
    state = pltpu.make_async_copy(x_ref, x, sems.at[steps])
    state.start()
    reads = [
        pltpu.make_async_copy(l_ref.at[:, pl.ds(step * width, width)], blocks.at[step], sems.at[step])
        for step in range(steps)
    ]
    for read in reads:
        read.start()
    state.wait()
    iterate_singly(POLAR - EARLY, x, a, b, r)
    updated = (x[...] * math.sqrt(n)).T
    left_form(a, updated)
    x[...] = updated
    count = columns_ref.shape[0]
    columns_ref[...] = x[pl.ds(pl.multiple_of(scalars[1] * count, count), count)]
    per_step = width // n

    def write(w):
        return pltpu.make_async_copy(result.at[w], o_ref.at[w], out_sems.at[w])

    def pair(step, carry):
        columns = pl.ds(pl.multiple_of(step * width, width), width)
        pltpu.make_async_copy(l_ref.at[:, columns], blocks.at[step], sems.at[step]).wait()
        product = mm(a[...], blocks[step])
        for k in range(per_step):
            w = step * per_step + k
            left_form(result.at[w], product[:, k * n : (k + 1) * n])
            write(w).start()
        return carry

    lax.fori_loop(0, steps, pair, 0)
    for w in range(steps * per_step):
        write(w).wait()


def own_finish(scalars, iterate, stacked_left):
    n = iterate.shape[0]
    k = stacked_left.shape[1] // n
    hbm = pl.BlockSpec(memory_space=pltpu.HBM)
    return pl.pallas_call(
        own_finish_kernel,
        out_shape=(jax.ShapeDtypeStruct((n // GROUPS, n), F32), jax.ShapeDtypeStruct((k, n, 3 * n), BF16)),
        in_specs=[pl.BlockSpec(memory_space=pltpu.SMEM), hbm, hbm],
        out_specs=(WHOLE, hbm),
        scratch_shapes=polar_scratch(n)
        + [
            pltpu.VMEM((k // 2, 3 * n, 2 * n), BF16),
            pltpu.VMEM((k, n, 3 * n), BF16),
            pltpu.SemaphoreType.DMA((k // 2 + 1,)),
            pltpu.SemaphoreType.DMA((k,)),
        ],
        compiler_params=params(),
        cost_estimate=cost(((POLAR - EARLY) * 12 + 6 * k) * n**3, 14 * k * n * n),
        name="own_finish",
    )(scalars, iterate, stacked_left)


def source_kernel(scalars, p_ref, h_ref, o_ref, x, a, b, r, g, mine, other, blocks, result, sems, out_sems):
    n = x.shape[0]
    operators = blocks.shape[0]
    reads = [pltpu.make_async_copy(h_ref.at[w], blocks.at[w], sems.at[w]) for w in range(operators)]
    for read in reads:
        read.start()
    pieces, count, _ = p_ref.shape
    chips, part = pieces // SECTORS, count // 2
    for piece in range(pieces):
        start = (piece % chips * SECTORS + piece // chips) * part
        mine[start : start + part] = p_ref[piece, 0:part]
        other[start : start + part] = p_ref[piece, part:count]
    lines, rows = mine.shape[0] // chips, n // GROUPS
    parts = []
    for ref, first in zip((mine, other), half_starts(scalars[0], n // 2), strict=True):
        for chip in range(chips):
            parts.append((ref.at[chip * lines : (chip + 1) * lines], first + chip * rows))
    start_polar(parts, x)
    iterate_polar(POLAR, x, a, b, r, g)
    right_form(r, x[...] * math.sqrt(n))

    def write(w):
        return pltpu.make_async_copy(result.at[w], o_ref.at[w], out_sems.at[w])

    def operator(w, carry):
        pltpu.make_async_copy(h_ref.at[w], blocks.at[w], sems.at[w]).wait()
        result[w] = mm(blocks[w], r[...])
        write(w).start()
        return carry

    lax.fori_loop(0, operators, operator, 0)
    for w in range(operators):
        write(w).wait()


def rotate_by_source(scalars, pieces, half3):
    k, n, _ = half3.shape
    half_lines = pltpu.VMEM((n * n // LANES // 2, LANES), F32)
    hbm = pl.BlockSpec(memory_space=pltpu.HBM)
    return pl.pallas_call(
        source_kernel,
        out_shape=jax.ShapeDtypeStruct((k, n, n), F32),
        in_specs=[pl.BlockSpec(memory_space=pltpu.SMEM), WHOLE, hbm],
        out_specs=hbm,
        scratch_shapes=polar_scratch(n)
        + [
            half_lines,
            half_lines,
            pltpu.VMEM((k, n, 3 * n), BF16),
            pltpu.VMEM((k, n, n), F32),
            pltpu.SemaphoreType.DMA((k,)),
            pltpu.SemaphoreType.DMA((k,)),
        ],
        compiler_params=params(),
        cost_estimate=cost((POLAR * 12 + 6 * k) * n**3, 10 * k * n * n),
        name="rotate_by_source",
    )(scalars, pieces, half3)


def cut_kernel(chip_ref, w_ref, o_ref, block, part, sem):
    rows = block.shape[0]
    here = pl.ds(pl.multiple_of(chip_ref[0] * rows, rows), rows)
    copy = pltpu.make_async_copy(w_ref.at[here], block, sem)
    copy.start()
    copy.wait()
    lines_of(part, block)
    pieces, count, _ = o_ref.shape
    for piece in range(pieces):
        o_ref[piece] = part[piece * count : (piece + 1) * count]


def cut(chip, block, chips):
    n = block.shape[0]
    rows = n // chips
    lines = rows * n // LANES
    return pl.pallas_call(
        cut_kernel,
        out_shape=jax.ShapeDtypeStruct((SECTORS, lines // SECTORS, LANES), F32),
        in_specs=[pl.BlockSpec(memory_space=pltpu.SMEM), pl.BlockSpec(memory_space=pltpu.HBM)],
        out_specs=WHOLE,
        scratch_shapes=[pltpu.VMEM((rows, n), F32), pltpu.VMEM((lines, LANES), F32), pltpu.SemaphoreType.DMA],
        compiler_params=params(ALL_VMEM),
        cost_estimate=cost(rows * n, 8 * rows * n),
        name="cut",
    )(chip, block)


def pair_kernel(mine_ref, other_ref, o_ref):
    pieces, count, _ = o_ref.shape
    part = count // 2
    for piece in range(pieces):
        lines = slice(piece * part, (piece + 1) * part)
        o_ref[piece, 0:part] = mine_ref[lines]
        o_ref[piece, part:count] = other_ref[lines]


def pair_up(mine, other):
    lines = mine.shape[0]
    return pl.pallas_call(
        pair_kernel,
        out_shape=jax.ShapeDtypeStruct((SECTORS, 2 * lines // SECTORS, LANES), F32),
        in_specs=[WHOLE, WHOLE],
        out_specs=WHOLE,
        compiler_params=params(),
        cost_estimate=cost(lines, 16 * lines * LANES),
        name="pair_up",
    )(mine, other)


def from_chips(block):
    chips = lax.axis_size("x")
    return [block] + [
        lax.ppermute(block, "x", [(j, (j - ahead) % chips) for j in range(chips)]) for ahead in range(1, chips)
    ]


def swap_cores(block):
    return lax.ppermute(block, "core", [(0, 1), (1, 0)])


def exchange(pieces, axes):
    return lax.all_to_all(pieces, axes, split_axis=0, concat_axis=0, tiled=True)


def deliver(spread, readers):
    return exchange(jnp.take(spread, readers, axis=0, mode="clip"), ("sector", "x"))


def shards(wavefunction, left_env, right_env, shift_map, op_counts):
    chips = lax.axis_size("x")
    chip, core = lax.axis_index("x"), lax.axis_index("core")
    group_here = chip * lax.axis_size("core") + core
    n = wavefunction.shape[1]
    lines = n * n // LANES
    scalars = jnp.stack([op_counts[0, 0], core.astype(jnp.int32)])
    readers = lax.all_gather(shift_map[0], "x").T.reshape(-1)
    left3, right3, stacked_left = prepare(left_env[0], right_env[0])

    spread = exchange(cut(chip.astype(jnp.int32)[None], wavefunction[0], chips), "sector")
    moved = deliver(spread, readers)

    own, other = partial_sigma(scalars, moved, left3, right3)
    pair = (own + swap_cores(other)).reshape(chips, lines // 2 // chips, LANES)
    chunk = jnp.sum(exchange(pair, "x"), axis=0)

    other_chunk = swap_cores(chunk)
    pieces = pair_up(chunk, other_chunk)
    spread = exchange(pieces, "sector")

    where = jnp.stack([core, group_here, chip]).astype(jnp.int32)
    mine = join(pieces, from_chips(chunk))
    early, spread = lax.optimization_barrier((own_start(where, mine, swap_cores(mine), n), spread))
    source_pieces = deliver(spread, readers)
    own_rows, half3 = own_finish(where, early, stacked_left)
    half3, source_pieces = lax.optimization_barrier((half3, source_pieces))
    rotated = rotate_by_source(where, source_pieces, half3)
    return (own_rows.T[None], rotated[None])


def solution(mesh):
    sectors, groups = mesh.devices.shape
    fine = Mesh(mesh.devices.reshape(sectors, groups // 2, 2), ("sector", "x", "core"))
    ops = ("x", "core")
    return jax.shard_map(
        shards,
        mesh=fine,
        in_specs=(
            P("sector", None, None),
            P("sector", ops, None, None),
            P("sector", ops, None, None),
            P(ops, None),
            P(ops, "sector"),
        ),
        out_specs=(P("sector", None, ops), P("sector", ops, None, None)),
        check_vma=False,
    )
```

```python
import functools
import math

import jax
import jax.numpy as jnp
from jax import lax
from jax.experimental import pallas as pl
from jax.experimental.pallas import tpu as pltpu
from jax.sharding import Mesh
from jax.sharding import PartitionSpec as P

POLAR = 5
SECTORS = 16
GROUPS = 8
EARLY = 1
LANES = 128
F32, BF16 = jnp.float32, jnp.bfloat16
VMEM_LIMIT = 48 << 20
ALL_VMEM = 58 << 20
WHOLE = pl.BlockSpec(memory_space=pltpu.VMEM)


def halves(v):
    high = v.astype(BF16)
    return high, (v - high.astype(F32)).astype(BF16)


def side_by_side(ref, a, b, c):
    n = a.shape[1]
    ref[:, 0:n] = a
    ref[:, n : 2 * n] = b
    ref[:, 2 * n : 3 * n] = c


def stacked(ref, a, b, c):
    n = a.shape[0]
    ref[0:n] = a
    ref[n : 2 * n] = b
    ref[2 * n : 3 * n] = c


def left_form(ref, v):
    high, low = halves(v)
    side_by_side(ref, high, high, low)


def right_form(ref, v):
    high, low = halves(v)
    stacked(ref, high, low, high)


def mm(a, b):
    return jnp.dot(a, b, preferred_element_type=F32)


def mm_nt(a, b):
    return lax.dot_general(a, b, (((1,), (1,)), ((), ())), preferred_element_type=F32)


def params(limit=VMEM_LIMIT):
    return pltpu.CompilerParams(vmem_limit_bytes=limit)


def cost(flops, nbytes):
    return pl.CostEstimate(flops=int(flops), bytes_accessed=int(nbytes), transcendentals=0)


def prepare_kernel(l_ref, r_ref, lo_ref, ro_ref, ls_ref):
    left_form(lo_ref.at[0], l_ref[0])
    right_form(ls_ref, l_ref[0])
    right_form(ro_ref.at[0], r_ref[0])


def prepare(left, right):
    k, n, _ = left.shape
    block = pl.BlockSpec((1, n, n), lambda w: (w, 0, 0))
    return pl.pallas_call(
        prepare_kernel,
        grid=(k,),
        out_shape=(
            jax.ShapeDtypeStruct((k, n, 3 * n), BF16),
            jax.ShapeDtypeStruct((k, 3 * n, n), BF16),
            jax.ShapeDtypeStruct((3 * n, k * n), BF16),
        ),
        in_specs=[block, block],
        out_specs=(
            pl.BlockSpec((1, n, 3 * n), lambda w: (w, 0, 0)),
            pl.BlockSpec((1, 3 * n, n), lambda w: (w, 0, 0)),
            pl.BlockSpec((3 * n, n), lambda w: (0, w)),
        ),
        compiler_params=params(),
        cost_estimate=cost(12 * k * n * n, 26 * k * n * n),
        name="prepare",
    )(left, right)


def tiles(n):
    return [(t, slice(t * LANES, (t + 1) * LANES)) for t in range(n // LANES)]


def lines_of(ref, v):
    count = v.shape[0]
    for t, lanes in tiles(v.shape[1]):
        ref[t * count : (t + 1) * count] = v[:, lanes]


def half_starts(core, half):
    return pl.multiple_of(core * half, half), pl.multiple_of((1 - core) * half, half)


def sigma_kernel(scalars, w_ref, l_ref, r_ref, own_ref, other_ref, w3, mid, acc, lines, left, right, l_sems, r_sems):
    n = acc.shape[0]
    operators = left.shape[0]

    def reads(w):
        return (
            pltpu.make_async_copy(l_ref.at[w], left.at[w], l_sems.at[w]),
            pltpu.make_async_copy(r_ref.at[w], right.at[w], r_sems.at[w]),
        )

    def arrived(w, carry=0):
        for read in reads(w):
            read.wait()
        return carry

    for w in range(operators):
        for read in reads(w):
            read.start()
    pieces, count, _ = w_ref.shape
    chips = pieces // SECTORS
    for piece in range(pieces):
        start = (piece % chips * SECTORS + piece // chips) * count
        lines[start : start + count] = w_ref[piece]
    part = n // chips
    for chip in range(chips):
        for t, lanes in tiles(n):
            start = chip * SECTORS * count + t * part
            high, low = halves(lines[start : start + part])
            for third, v in enumerate((high, low, high)):
                w3[third * n + chip * part : third * n + (chip + 1) * part, lanes] = v
    acc[...] = jnp.zeros_like(acc)

    def operator(w, carry):
        arrived(w)
        left_form(mid, mm(left[w], w3[...]))
        acc[...] += mm(mid[...], right[w])
        return carry

    lax.fori_loop(0, scalars[0], operator, 0)
    lax.fori_loop(scalars[0], operators, arrived, 0)
    chunk = n // GROUPS
    count = chunk * n // LANES
    for ref, start in zip((own_ref, other_ref), half_starts(scalars[1], n // 2), strict=True):
        for chip in range(GROUPS // 2):
            rows = pl.ds(pl.multiple_of(start + chip * chunk, chunk), chunk)
            lines_of(ref.at[chip * count : (chip + 1) * count], acc[rows])


def partial_sigma(scalars, pieces, left3, right3):
    k, n = left3.shape[:2]
    lines = n * n // LANES
    hbm = pl.BlockSpec(memory_space=pltpu.HBM)
    return pl.pallas_call(
        sigma_kernel,
        out_shape=(jax.ShapeDtypeStruct((lines // 2, LANES), F32),) * 2,
        in_specs=[pl.BlockSpec(memory_space=pltpu.SMEM), WHOLE, hbm, hbm],
        out_specs=(WHOLE, WHOLE),
        scratch_shapes=[
            pltpu.VMEM((3 * n, n), BF16),
            pltpu.VMEM((n, 3 * n), BF16),
            pltpu.VMEM((n, n), F32),
            pltpu.VMEM((lines, LANES), F32),
            pltpu.VMEM((k, n, 3 * n), BF16),
            pltpu.VMEM((k, 3 * n, n), BF16),
            pltpu.SemaphoreType.DMA((k,)),
            pltpu.SemaphoreType.DMA((k,)),
        ],
        compiler_params=params(),
        cost_estimate=cost(12 * k * n**3, 16 * k * n * n),
        name="partial_sigma",
    )(scalars, pieces, left3, right3)


def start_polar(parts, x):
    n = x.shape[0]
    total = sum(jnp.sum(lines[...] * lines[...]) for lines, _ in parts)
    factor = lax.rsqrt(n * (total / float(n * n)) + 1e-06) / 2.2
    for lines, start in parts:
        count = lines.shape[0] * LANES // n
        rows = pl.ds(pl.multiple_of(start, count), count)
        for t, lanes in tiles(n):
            x[rows, lanes] = lines[t * count : (t + 1) * count] * factor


def symmetric_rows(a, b):
    n = a.shape[0]
    first = mm_nt(a[...], b[0:256])
    second = mm_nt(a[256:n], b[256:512])
    third = mm_nt(a[512:n], b[512:n])
    return (
        (slice(0, 256), jnp.concatenate((first[0:256], first[256:n].T), 1)),
        (slice(256, 512), jnp.concatenate((first[256:512], second[0:256], second[256 : n - 256].T), 1)),
        (slice(512, n), jnp.concatenate((first[512:n], second[256 : n - 256], third), 1)),
    )


def split_iterate(x, a, b, r):
    high, low = halves(x[...])
    side_by_side(a, high, high, low)
    side_by_side(b, high, low, high)
    stacked(r, high, low, high)


def iterate_once(x, a, b, r):
    split_iterate(x, a, b, r)
    for rows, v in symmetric_rows(a, b):
        left_form(a.at[rows], v)
    x[...] = 1.5 * x[...] - 0.5 * mm(a[...], r[...])


def iterate_twice(x, a, b, r, g):
    split_iterate(x, a, b, r)
    for rows, v in symmetric_rows(a, b):
        g[rows] = v
    high, low = halves(g[...])
    side_by_side(a, high, high, low)
    side_by_side(b, high, low, high)
    n = x.shape[0]
    for rows, q in symmetric_rows(a, b):
        gram = g[rows]
        left_form(a.at[rows], q)
        high, low = halves(0.0625 * q - 0.5625 * gram)
        side_by_side(b.at[rows], high, low, high)
        row = lax.broadcasted_iota(jnp.int32, q.shape, 0) + rows.start
        diagonal = row == lax.broadcasted_iota(jnp.int32, q.shape, 1)
        g[rows] = 1.6875 * q - 2.4375 * gram + jnp.where(diagonal, 2.25, 0.0)
    for rows, v in symmetric_rows(a, b):
        left_form(a.at[rows], g[rows] + v)
    x[...] = mm(a[...], r[...])


def iterate_polar(iterations, x, a, b, r, g):
    def twice(_, carry):
        iterate_twice(x, a, b, r, g)
        return carry

    lax.fori_loop(0, iterations // 2, twice, 0)
    if iterations % 2:
        iterate_once(x, a, b, r)


def iterate_singly(iterations, x, a, b, r):
    def once(_, carry):
        iterate_once(x, a, b, r)
        return carry

    lax.fori_loop(0, iterations, once, 0)


def polar_scratch(n):
    return [
        pltpu.VMEM((n, n), F32),
        pltpu.VMEM((n, 3 * n), BF16),
        pltpu.VMEM((n, 3 * n), BF16),
        pltpu.VMEM((3 * n, n), BF16),
        pltpu.VMEM((n, n), F32),
    ]


def own_start_kernel(scalars, *refs):
    gathered, (o_ref, x, a, b, r, _, sem) = refs[:GROUPS], refs[GROUPS:]
    n = x.shape[0]
    chips = GROUPS // 2
    parts = []
    for core, first in enumerate(half_starts(scalars[0], n // 2)):
        for ahead in range(chips):
            start = first + lax.rem(scalars[2] + ahead, chips) * (n // GROUPS)
            parts.append((gathered[core * chips + ahead], start))
    start_polar(parts, x)
    iterate_singly(EARLY, x, a, b, r)
    copy = pltpu.make_async_copy(x, o_ref, sem)
    copy.start()
    copy.wait()


def own_start(scalars, gathered, n):
    return pl.pallas_call(
        own_start_kernel,
        out_shape=jax.ShapeDtypeStruct((n, n), F32),
        in_specs=[pl.BlockSpec(memory_space=pltpu.SMEM)] + [WHOLE] * GROUPS,
        out_specs=pl.BlockSpec(memory_space=pltpu.HBM),
        scratch_shapes=polar_scratch(n) + [pltpu.SemaphoreType.DMA],
        compiler_params=params(ALL_VMEM),
        cost_estimate=cost(EARLY * 12 * n**3, 8 * n * n),
        name="own_start",
    )(scalars, *gathered)


def own_finish_kernel(scalars, x_ref, l_ref, columns_ref, o_ref, x, a, b, r, g, blocks, result, sems, out_sems):
    n = x.shape[0]
    steps, _, width = blocks.shape
    state = pltpu.make_async_copy(x_ref, x, sems.at[steps])
    state.start()
    reads = [
        pltpu.make_async_copy(l_ref.at[:, pl.ds(step * width, width)], blocks.at[step], sems.at[step])
        for step in range(steps)
    ]
    for read in reads:
        read.start()
    state.wait()
    iterate_singly(POLAR - EARLY, x, a, b, r)
    updated = (x[...] * math.sqrt(n)).T
    left_form(a, updated)
    x[...] = updated
    count = columns_ref.shape[0]
    columns_ref[...] = x[pl.ds(pl.multiple_of(scalars[1] * count, count), count)]
    per_step = width // n

    def write(w):
        return pltpu.make_async_copy(result.at[w], o_ref.at[w], out_sems.at[w])

    def pair(step, carry):
        columns = pl.ds(pl.multiple_of(step * width, width), width)
        pltpu.make_async_copy(l_ref.at[:, columns], blocks.at[step], sems.at[step]).wait()
        product = mm(a[...], blocks[step])
        for k in range(per_step):
            w = step * per_step + k
            left_form(result.at[w], product[:, k * n : (k + 1) * n])
            write(w).start()
        return carry

    lax.fori_loop(0, steps, pair, 0)
    for w in range(steps * per_step):
        write(w).wait()


def own_finish(scalars, iterate, stacked_left):
    n = iterate.shape[0]
    k = stacked_left.shape[1] // n
    hbm = pl.BlockSpec(memory_space=pltpu.HBM)
    return pl.pallas_call(
        own_finish_kernel,
        out_shape=(jax.ShapeDtypeStruct((n // GROUPS, n), F32), jax.ShapeDtypeStruct((k, n, 3 * n), BF16)),
        in_specs=[pl.BlockSpec(memory_space=pltpu.SMEM), hbm, hbm],
        out_specs=(WHOLE, hbm),
        scratch_shapes=polar_scratch(n)
        + [
            pltpu.VMEM((k // 2, 3 * n, 2 * n), BF16),
            pltpu.VMEM((k, n, 3 * n), BF16),
            pltpu.SemaphoreType.DMA((k // 2 + 1,)),
            pltpu.SemaphoreType.DMA((k,)),
        ],
        compiler_params=params(),
        cost_estimate=cost(((POLAR - EARLY) * 12 + 6 * k) * n**3, 14 * k * n * n),
        name="own_finish",
    )(scalars, iterate, stacked_left)


def source_kernel(scalars, p_ref, h_ref, o_ref, x, a, b, r, g, mine, other, blocks, result, sems, out_sems):
    n = x.shape[0]
    operators = blocks.shape[0]
    reads = [pltpu.make_async_copy(h_ref.at[w], blocks.at[w], sems.at[w]) for w in range(operators)]
    for read in reads:
        read.start()
    pieces, count, _ = p_ref.shape
    chips, part = pieces // SECTORS, count // 2
    for piece in range(pieces):
        start = (piece % chips * SECTORS + piece // chips) * part
        mine[start : start + part] = p_ref[piece, 0:part]
        other[start : start + part] = p_ref[piece, part:count]
    lines, rows = mine.shape[0] // chips, n // GROUPS
    parts = []
    for ref, first in zip((mine, other), half_starts(scalars[0], n // 2), strict=True):
        for chip in range(chips):
            parts.append((ref.at[chip * lines : (chip + 1) * lines], first + chip * rows))
    start_polar(parts, x)
    iterate_polar(POLAR, x, a, b, r, g)
    right_form(r, x[...] * math.sqrt(n))

    def write(w):
        return pltpu.make_async_copy(result.at[w], o_ref.at[w], out_sems.at[w])

    def operator(w, carry):
        pltpu.make_async_copy(h_ref.at[w], blocks.at[w], sems.at[w]).wait()
        result[w] = mm(blocks[w], r[...])
        write(w).start()
        return carry

    lax.fori_loop(0, operators, operator, 0)
    for w in range(operators):
        write(w).wait()


def rotate_by_source(scalars, pieces, half3):
    k, n, _ = half3.shape
    half_lines = pltpu.VMEM((n * n // LANES // 2, LANES), F32)
    hbm = pl.BlockSpec(memory_space=pltpu.HBM)
    return pl.pallas_call(
        source_kernel,
        out_shape=jax.ShapeDtypeStruct((k, n, n), F32),
        in_specs=[pl.BlockSpec(memory_space=pltpu.SMEM), WHOLE, hbm],
        out_specs=hbm,
        scratch_shapes=polar_scratch(n)
        + [
            half_lines,
            half_lines,
            pltpu.VMEM((k, n, 3 * n), BF16),
            pltpu.VMEM((k, n, n), F32),
            pltpu.SemaphoreType.DMA((k,)),
            pltpu.SemaphoreType.DMA((k,)),
        ],
        compiler_params=params(),
        cost_estimate=cost((POLAR * 12 + 6 * k) * n**3, 10 * k * n * n),
        name="rotate_by_source",
    )(scalars, pieces, half3)


def cut_kernel(chip_ref, w_ref, o_ref, block, part, sem):
    rows = block.shape[0]
    here = pl.ds(pl.multiple_of(chip_ref[0] * rows, rows), rows)
    copy = pltpu.make_async_copy(w_ref.at[here], block, sem)
    copy.start()
    copy.wait()
    lines_of(part, block)
    pieces, count, _ = o_ref.shape
    for piece in range(pieces):
        o_ref[piece] = part[piece * count : (piece + 1) * count]


def cut(chip, block, chips):
    n = block.shape[0]
    rows = n // chips
    lines = rows * n // LANES
    return pl.pallas_call(
        cut_kernel,
        out_shape=jax.ShapeDtypeStruct((SECTORS, lines // SECTORS, LANES), F32),
        in_specs=[pl.BlockSpec(memory_space=pltpu.SMEM), pl.BlockSpec(memory_space=pltpu.HBM)],
        out_specs=WHOLE,
        scratch_shapes=[pltpu.VMEM((rows, n), F32), pltpu.VMEM((lines, LANES), F32), pltpu.SemaphoreType.DMA],
        compiler_params=params(ALL_VMEM),
        cost_estimate=cost(rows * n, 8 * rows * n),
        name="cut",
    )(chip, block)


def pair_kernel(mine_ref, other_ref, o_ref):
    pieces, count, _ = o_ref.shape
    part = count // 2
    for piece in range(pieces):
        lines = slice(piece * part, (piece + 1) * part)
        o_ref[piece, 0:part] = mine_ref[lines]
        o_ref[piece, part:count] = other_ref[lines]


def pair_up(mine, other):
    lines = mine.shape[0]
    return pl.pallas_call(
        pair_kernel,
        out_shape=jax.ShapeDtypeStruct((SECTORS, 2 * lines // SECTORS, LANES), F32),
        in_specs=[WHOLE, WHOLE],
        out_specs=WHOLE,
        compiler_params=params(),
        cost_estimate=cost(lines, 16 * lines * LANES),
        name="pair_up",
    )(mine, other)


def from_chips(block):
    chips = lax.axis_size("x")
    return [block] + [
        lax.ppermute(block, "x", [(j, (j - ahead) % chips) for j in range(chips)]) for ahead in range(1, chips)
    ]


def swap_cores(block):
    return lax.ppermute(block, "core", [(0, 1), (1, 0)])


def exchange(pieces, axes):
    return lax.all_to_all(pieces, axes, split_axis=0, concat_axis=0, tiled=True)


def deliver(spread, readers):
    return exchange(jnp.take(spread, readers, axis=0, mode="clip"), ("sector", "x"))


def shards(wavefunction, left_env, right_env, shift_map, op_counts):
    chips = lax.axis_size("x")
    chip, core = lax.axis_index("x"), lax.axis_index("core")
    group_here = chip * lax.axis_size("core") + core
    n = wavefunction.shape[1]
    lines = n * n // LANES
    scalars = jnp.stack([op_counts[0, 0], core.astype(jnp.int32)])
    readers = lax.all_gather(shift_map[0], "x").T.reshape(-1)
    left3, right3, stacked_left = prepare(left_env[0], right_env[0])

    spread = exchange(cut(chip.astype(jnp.int32)[None], wavefunction[0], chips), "sector")
    moved = deliver(spread, readers)

    own, other = partial_sigma(scalars, moved, left3, right3)
    pair = (own + swap_cores(other)).reshape(chips, lines // 2 // chips, LANES)
    chunk = jnp.sum(exchange(pair, "x"), axis=0)

    other_chunk = swap_cores(chunk)
    spread = exchange(pair_up(chunk, other_chunk), "sector")

    where = jnp.stack([core, group_here, chip]).astype(jnp.int32)
    gathered = from_chips(chunk) + from_chips(other_chunk)
    early, spread = lax.optimization_barrier((own_start(where, gathered, n), spread))
    source_pieces = deliver(spread, readers)
    own_rows, half3 = own_finish(where, early, stacked_left)
    half3, source_pieces = lax.optimization_barrier((half3, source_pieces))
    rotated = rotate_by_source(where, source_pieces, half3)
    return (own_rows.T[None], rotated[None])


def solution(mesh):
    sectors, groups = mesh.devices.shape
    fine = Mesh(mesh.devices.reshape(sectors, groups // 2, 2), ("sector", "x", "core"))
    ops = ("x", "core")
    return jax.shard_map(
        shards,
        mesh=fine,
        in_specs=(
            P("sector", None, None),
            P("sector", ops, None, None),
            P("sector", ops, None, None),
            P(ops, None),
            P(ops, "sector"),
        ),
        out_specs=(P("sector", None, ops), P("sector", ops, None, None)),
        check_vma=False,
    )
```

```python
import functools
import math

import jax
import jax.numpy as jnp
from jax import lax
from jax.experimental import pallas as pl
from jax.experimental.pallas import tpu as pltpu
from jax.sharding import Mesh
from jax.sharding import PartitionSpec as P

POLAR = 5
SECTORS = 16
GROUPS = 8
EARLY = 1
LANES = 128
F32, BF16 = jnp.float32, jnp.bfloat16
VMEM_LIMIT = 48 << 20
ALL_VMEM = 58 << 20
WHOLE = pl.BlockSpec(memory_space=pltpu.VMEM)


def halves(v):
    high = v.astype(BF16)
    return high, (v - high.astype(F32)).astype(BF16)


def side_by_side(ref, a, b, c):
    n = a.shape[1]
    ref[:, 0:n] = a
    ref[:, n : 2 * n] = b
    ref[:, 2 * n : 3 * n] = c


def stacked(ref, a, b, c):
    n = a.shape[0]
    ref[0:n] = a
    ref[n : 2 * n] = b
    ref[2 * n : 3 * n] = c


def left_form(ref, v):
    high, low = halves(v)
    side_by_side(ref, high, high, low)


def right_form(ref, v):
    high, low = halves(v)
    stacked(ref, high, low, high)


def mm(a, b):
    return jnp.dot(a, b, preferred_element_type=F32)


def mm_nt(a, b):
    return lax.dot_general(a, b, (((1,), (1,)), ((), ())), preferred_element_type=F32)


def params(limit=VMEM_LIMIT):
    return pltpu.CompilerParams(vmem_limit_bytes=limit)


def cost(flops, nbytes):
    return pl.CostEstimate(flops=int(flops), bytes_accessed=int(nbytes), transcendentals=0)


def prepare_kernel(l_ref, r_ref, lo_ref, ro_ref, ls_ref):
    left_form(lo_ref.at[0], l_ref[0])
    right_form(ls_ref, l_ref[0])
    right_form(ro_ref.at[0], r_ref[0])


def prepare(left, right):
    k, n, _ = left.shape
    block = pl.BlockSpec((1, n, n), lambda w: (w, 0, 0))
    return pl.pallas_call(
        prepare_kernel,
        grid=(k,),
        out_shape=(
            jax.ShapeDtypeStruct((k, n, 3 * n), BF16),
            jax.ShapeDtypeStruct((k, 3 * n, n), BF16),
            jax.ShapeDtypeStruct((3 * n, k * n), BF16),
        ),
        in_specs=[block, block],
        out_specs=(
            pl.BlockSpec((1, n, 3 * n), lambda w: (w, 0, 0)),
            pl.BlockSpec((1, 3 * n, n), lambda w: (w, 0, 0)),
            pl.BlockSpec((3 * n, n), lambda w: (0, w)),
        ),
        compiler_params=params(),
        cost_estimate=cost(12 * k * n * n, 26 * k * n * n),
        name="prepare",
    )(left, right)


def tiles(n):
    return [(t, slice(t * LANES, (t + 1) * LANES)) for t in range(n // LANES)]


def lines_of(ref, v):
    count = v.shape[0]
    for t, lanes in tiles(v.shape[1]):
        ref[t * count : (t + 1) * count] = v[:, lanes]


def half_starts(core, half):
    return pl.multiple_of(core * half, half), pl.multiple_of((1 - core) * half, half)


def sigma_kernel(scalars, w_ref, l_ref, r_ref, own_ref, other_ref, w3, mid, acc, lines, left, right, l_sems, r_sems):
    n = acc.shape[0]
    operators = left.shape[0]

    def reads(w):
        return (
            pltpu.make_async_copy(l_ref.at[w], left.at[w], l_sems.at[w]),
            pltpu.make_async_copy(r_ref.at[w], right.at[w], r_sems.at[w]),
        )

    def arrived(w, carry=0):
        for read in reads(w):
            read.wait()
        return carry

    for w in range(operators):
        for read in reads(w):
            read.start()
    pieces, count, _ = w_ref.shape
    chips = pieces // SECTORS
    for piece in range(pieces):
        start = (piece % chips * SECTORS + piece // chips) * count
        lines[start : start + count] = w_ref[piece]
    part = n // chips
    for chip in range(chips):
        for t, lanes in tiles(n):
            start = chip * SECTORS * count + t * part
            high, low = halves(lines[start : start + part])
            for third, v in enumerate((high, low, high)):
                w3[third * n + chip * part : third * n + (chip + 1) * part, lanes] = v
    acc[...] = jnp.zeros_like(acc)

    def operator(w, carry):
        arrived(w)
        left_form(mid, mm(left[w], w3[...]))
        acc[...] += mm(mid[...], right[w])
        return carry

    lax.fori_loop(0, scalars[0], operator, 0)
    lax.fori_loop(scalars[0], operators, arrived, 0)
    chunk = n // GROUPS
    count = chunk * n // LANES
    for ref, start in zip((own_ref, other_ref), half_starts(scalars[1], n // 2), strict=True):
        for chip in range(GROUPS // 2):
            rows = pl.ds(pl.multiple_of(start + chip * chunk, chunk), chunk)
            lines_of(ref.at[chip * count : (chip + 1) * count], acc[rows])


def partial_sigma(scalars, pieces, left3, right3):
    k, n = left3.shape[:2]
    lines = n * n // LANES
    hbm = pl.BlockSpec(memory_space=pltpu.HBM)
    return pl.pallas_call(
        sigma_kernel,
        out_shape=(jax.ShapeDtypeStruct((lines // 2, LANES), F32),) * 2,
        in_specs=[pl.BlockSpec(memory_space=pltpu.SMEM), WHOLE, hbm, hbm],
        out_specs=(WHOLE, WHOLE),
        scratch_shapes=[
            pltpu.VMEM((3 * n, n), BF16),
            pltpu.VMEM((n, 3 * n), BF16),
            pltpu.VMEM((n, n), F32),
            pltpu.VMEM((lines, LANES), F32),
            pltpu.VMEM((k, n, 3 * n), BF16),
            pltpu.VMEM((k, 3 * n, n), BF16),
            pltpu.SemaphoreType.DMA((k,)),
            pltpu.SemaphoreType.DMA((k,)),
        ],
        compiler_params=params(),
        cost_estimate=cost(12 * k * n**3, 16 * k * n * n),
        name="partial_sigma",
    )(scalars, pieces, left3, right3)


def start_polar(parts, x):
    n = x.shape[0]
    total = sum(jnp.sum(lines[...] * lines[...]) for lines, _ in parts)
    factor = lax.rsqrt(n * (total / float(n * n)) + 1e-06) / 2.2
    for lines, start in parts:
        count = lines.shape[0] * LANES // n
        rows = pl.ds(pl.multiple_of(start, count), count)
        for t, lanes in tiles(n):
            x[rows, lanes] = lines[t * count : (t + 1) * count] * factor


def symmetric_rows(a, b):
    n = a.shape[0]
    first = mm_nt(a[...], b[0:256])
    second = mm_nt(a[256:n], b[256:512])
    third = mm_nt(a[512:n], b[512:n])
    return (
        (slice(0, 256), jnp.concatenate((first[0:256], first[256:n].T), 1)),
        (slice(256, 512), jnp.concatenate((first[256:512], second[0:256], second[256 : n - 256].T), 1)),
        (slice(512, n), jnp.concatenate((first[512:n], second[256 : n - 256], third), 1)),
    )


def split_iterate(x, a, b, r):
    high, low = halves(x[...])
    side_by_side(a, high, high, low)
    side_by_side(b, high, low, high)
    stacked(r, high, low, high)


def iterate_once(x, a, b, r):
    split_iterate(x, a, b, r)
    for rows, v in symmetric_rows(a, b):
        left_form(a.at[rows], v)
    x[...] = 1.5 * x[...] - 0.5 * mm(a[...], r[...])


def iterate_twice(x, a, b, r, g):
    split_iterate(x, a, b, r)
    for rows, v in symmetric_rows(a, b):
        g[rows] = v
    high, low = halves(g[...])
    side_by_side(a, high, high, low)
    side_by_side(b, high, low, high)
    n = x.shape[0]
    for rows, q in symmetric_rows(a, b):
        gram = g[rows]
        left_form(a.at[rows], q)
        high, low = halves(0.0625 * q - 0.5625 * gram)
        side_by_side(b.at[rows], high, low, high)
        row = lax.broadcasted_iota(jnp.int32, q.shape, 0) + rows.start
        diagonal = row == lax.broadcasted_iota(jnp.int32, q.shape, 1)
        g[rows] = 1.6875 * q - 2.4375 * gram + jnp.where(diagonal, 2.25, 0.0)
    for rows, v in symmetric_rows(a, b):
        left_form(a.at[rows], g[rows] + v)
    x[...] = mm(a[...], r[...])


def iterate_polar(iterations, x, a, b, r, g):
    def twice(_, carry):
        iterate_twice(x, a, b, r, g)
        return carry

    lax.fori_loop(0, iterations // 2, twice, 0)
    if iterations % 2:
        iterate_once(x, a, b, r)


def iterate_singly(iterations, x, a, b, r):
    def once(_, carry):
        iterate_once(x, a, b, r)
        return carry

    lax.fori_loop(0, iterations, once, 0)


def polar_scratch(n):
    return [
        pltpu.VMEM((n, n), F32),
        pltpu.VMEM((n, 3 * n), BF16),
        pltpu.VMEM((n, 3 * n), BF16),
        pltpu.VMEM((3 * n, n), BF16),
        pltpu.VMEM((n, n), F32),
    ]


def join_kernel(_, *refs):
    o_ref = refs[-1]
    lines = refs[0].shape[0]
    for k, ref in enumerate(refs[:-1]):
        o_ref[k * lines : (k + 1) * lines] = ref[...]


def join(after, blocks):
    lines, lanes = blocks[0].shape
    return pl.pallas_call(
        join_kernel,
        out_shape=jax.ShapeDtypeStruct((len(blocks) * lines, lanes), F32),
        in_specs=[pl.BlockSpec(memory_space=pltpu.HBM)] + [WHOLE] * len(blocks),
        out_specs=WHOLE,
        compiler_params=params(),
        cost_estimate=cost(lines, 8 * len(blocks) * lines * lanes),
        name="join",
    )(after, *blocks)


def own_start_kernel(scalars, mine_ref, other_ref, o_ref, x, a, b, r, _, sem):
    n = x.shape[0]
    chips = GROUPS // 2
    lines = mine_ref.shape[0] // chips
    parts = []
    for ref, first in zip((mine_ref, other_ref), half_starts(scalars[0], n // 2), strict=True):
        for ahead in range(chips):
            start = first + lax.rem(scalars[2] + ahead, chips) * (n // GROUPS)
            parts.append((ref.at[ahead * lines : (ahead + 1) * lines], start))
    start_polar(parts, x)
    iterate_singly(EARLY, x, a, b, r)
    copy = pltpu.make_async_copy(x, o_ref, sem)
    copy.start()
    copy.wait()


def own_start(scalars, mine, other, n):
    return pl.pallas_call(
        own_start_kernel,
        out_shape=jax.ShapeDtypeStruct((n, n), F32),
        in_specs=[pl.BlockSpec(memory_space=pltpu.SMEM), WHOLE, WHOLE],
        out_specs=pl.BlockSpec(memory_space=pltpu.HBM),
        scratch_shapes=polar_scratch(n) + [pltpu.SemaphoreType.DMA],
        compiler_params=params(ALL_VMEM),
        cost_estimate=cost(EARLY * 12 * n**3, 8 * n * n),
        name="own_start",
    )(scalars, mine, other)


def own_finish_kernel(scalars, x_ref, l_ref, columns_ref, o_ref, x, a, b, r, g, blocks, result, sems, out_sems):
    n = x.shape[0]
    steps, _, width = blocks.shape
    state = pltpu.make_async_copy(x_ref, x, sems.at[steps])
    state.start()
    reads = [
        pltpu.make_async_copy(l_ref.at[:, pl.ds(step * width, width)], blocks.at[step], sems.at[step])
        for step in range(steps)
    ]
    for read in reads:
        read.start()
    state.wait()
    iterate_singly(POLAR - EARLY, x, a, b, r)
    updated = (x[...] * math.sqrt(n)).T
    left_form(a, updated)
    x[...] = updated
    count = columns_ref.shape[0]
    columns_ref[...] = x[pl.ds(pl.multiple_of(scalars[1] * count, count), count)]
    per_step = width // n

    def write(w):
        return pltpu.make_async_copy(result.at[w], o_ref.at[w], out_sems.at[w])

    def pair(step, carry):
        columns = pl.ds(pl.multiple_of(step * width, width), width)
        pltpu.make_async_copy(l_ref.at[:, columns], blocks.at[step], sems.at[step]).wait()
        product = mm(a[...], blocks[step])
        for k in range(per_step):
            w = step * per_step + k
            left_form(result.at[w], product[:, k * n : (k + 1) * n])
            write(w).start()
        return carry

    lax.fori_loop(0, steps, pair, 0)
    for w in range(steps * per_step):
        write(w).wait()


def own_finish(scalars, iterate, stacked_left):
    n = iterate.shape[0]
    k = stacked_left.shape[1] // n
    hbm = pl.BlockSpec(memory_space=pltpu.HBM)
    return pl.pallas_call(
        own_finish_kernel,
        out_shape=(jax.ShapeDtypeStruct((n // GROUPS, n), F32), jax.ShapeDtypeStruct((k, n, 3 * n), BF16)),
        in_specs=[pl.BlockSpec(memory_space=pltpu.SMEM), hbm, hbm],
        out_specs=(WHOLE, hbm),
        scratch_shapes=polar_scratch(n)
        + [
            pltpu.VMEM((k // 2, 3 * n, 2 * n), BF16),
            pltpu.VMEM((k, n, 3 * n), BF16),
            pltpu.SemaphoreType.DMA((k // 2 + 1,)),
            pltpu.SemaphoreType.DMA((k,)),
        ],
        compiler_params=params(),
        cost_estimate=cost(((POLAR - EARLY) * 12 + 6 * k) * n**3, 14 * k * n * n),
        name="own_finish",
    )(scalars, iterate, stacked_left)


def source_kernel(scalars, p_ref, h_ref, o_ref, x, a, b, r, g, mine, other, blocks, result, sems, out_sems):
    n = x.shape[0]
    operators = blocks.shape[0]
    reads = [pltpu.make_async_copy(h_ref.at[w], blocks.at[w], sems.at[w]) for w in range(operators)]
    for read in reads:
        read.start()
    pieces, count, _ = p_ref.shape
    chips, part = pieces // SECTORS, count // 2
    for piece in range(pieces):
        start = (piece % chips * SECTORS + piece // chips) * part
        mine[start : start + part] = p_ref[piece, 0:part]
        other[start : start + part] = p_ref[piece, part:count]
    lines, rows = mine.shape[0] // chips, n // GROUPS
    parts = []
    for ref, first in zip((mine, other), half_starts(scalars[0], n // 2), strict=True):
        for chip in range(chips):
            parts.append((ref.at[chip * lines : (chip + 1) * lines], first + chip * rows))
    start_polar(parts, x)
    iterate_polar(POLAR, x, a, b, r, g)
    right_form(r, x[...] * math.sqrt(n))

    def write(w):
        return pltpu.make_async_copy(result.at[w], o_ref.at[w], out_sems.at[w])

    def operator(w, carry):
        pltpu.make_async_copy(h_ref.at[w], blocks.at[w], sems.at[w]).wait()
        result[w] = mm(blocks[w], r[...])
        write(w).start()
        return carry

    lax.fori_loop(0, operators, operator, 0)
    for w in range(operators):
        write(w).wait()


def rotate_by_source(scalars, pieces, half3):
    k, n, _ = half3.shape
    half_lines = pltpu.VMEM((n * n // LANES // 2, LANES), F32)
    hbm = pl.BlockSpec(memory_space=pltpu.HBM)
    return pl.pallas_call(
        source_kernel,
        out_shape=jax.ShapeDtypeStruct((k, n, n), F32),
        in_specs=[pl.BlockSpec(memory_space=pltpu.SMEM), WHOLE, hbm],
        out_specs=hbm,
        scratch_shapes=polar_scratch(n)
        + [
            half_lines,
            half_lines,
            pltpu.VMEM((k, n, 3 * n), BF16),
            pltpu.VMEM((k, n, n), F32),
            pltpu.SemaphoreType.DMA((k,)),
            pltpu.SemaphoreType.DMA((k,)),
        ],
        compiler_params=params(),
        cost_estimate=cost((POLAR * 12 + 6 * k) * n**3, 10 * k * n * n),
        name="rotate_by_source",
    )(scalars, pieces, half3)


def cut_kernel(chip_ref, w_ref, o_ref, block, part, sem):
    rows = block.shape[0]
    here = pl.ds(pl.multiple_of(chip_ref[0] * rows, rows), rows)
    copy = pltpu.make_async_copy(w_ref.at[here], block, sem)
    copy.start()
    copy.wait()
    lines_of(part, block)
    pieces, count, _ = o_ref.shape
    for piece in range(pieces):
        o_ref[piece] = part[piece * count : (piece + 1) * count]


def cut(chip, block, chips):
    n = block.shape[0]
    rows = n // chips
    lines = rows * n // LANES
    return pl.pallas_call(
        cut_kernel,
        out_shape=jax.ShapeDtypeStruct((SECTORS, lines // SECTORS, LANES), F32),
        in_specs=[pl.BlockSpec(memory_space=pltpu.SMEM), pl.BlockSpec(memory_space=pltpu.HBM)],
        out_specs=WHOLE,
        scratch_shapes=[pltpu.VMEM((rows, n), F32), pltpu.VMEM((lines, LANES), F32), pltpu.SemaphoreType.DMA],
        compiler_params=params(ALL_VMEM),
        cost_estimate=cost(rows * n, 8 * rows * n),
        name="cut",
    )(chip, block)


def pair_kernel(mine_ref, other_ref, o_ref):
    pieces, count, _ = o_ref.shape
    part = count // 2
    for piece in range(pieces):
        lines = slice(piece * part, (piece + 1) * part)
        o_ref[piece, 0:part] = mine_ref[lines]
        o_ref[piece, part:count] = other_ref[lines]


def pair_up(mine, other):
    lines = mine.shape[0]
    return pl.pallas_call(
        pair_kernel,
        out_shape=jax.ShapeDtypeStruct((SECTORS, 2 * lines // SECTORS, LANES), F32),
        in_specs=[WHOLE, WHOLE],
        out_specs=WHOLE,
        compiler_params=params(),
        cost_estimate=cost(lines, 16 * lines * LANES),
        name="pair_up",
    )(mine, other)


def from_chips(block):
    chips = lax.axis_size("x")
    return [block] + [
        lax.ppermute(block, "x", [(j, (j - ahead) % chips) for j in range(chips)]) for ahead in range(1, chips)
    ]


def swap_cores(block):
    return lax.ppermute(block, "core", [(0, 1), (1, 0)])


def exchange(pieces, axes):
    return lax.all_to_all(pieces, axes, split_axis=0, concat_axis=0, tiled=True)


def deliver(spread, readers):
    return exchange(jnp.take(spread, readers, axis=0, mode="clip"), ("sector", "x"))


def shards(wavefunction, left_env, right_env, shift_map, op_counts):
    chips = lax.axis_size("x")
    chip, core = lax.axis_index("x"), lax.axis_index("core")
    group_here = chip * lax.axis_size("core") + core
    n = wavefunction.shape[1]
    lines = n * n // LANES
    scalars = jnp.stack([op_counts[0, 0], core.astype(jnp.int32)])
    readers = lax.all_gather(shift_map[0], "x").T.reshape(-1)
    left3, right3, stacked_left = prepare(left_env[0], right_env[0])

    spread = exchange(cut(chip.astype(jnp.int32)[None], wavefunction[0], chips), "sector")
    moved = deliver(spread, readers)

    own, other = partial_sigma(scalars, moved, left3, right3)
    pair = (own + swap_cores(other)).reshape(chips, lines // 2 // chips, LANES)
    chunk = jnp.sum(exchange(pair, "x"), axis=0)

    other_chunk = swap_cores(chunk)
    pieces = pair_up(chunk, other_chunk)
    spread = exchange(pieces, "sector")

    where = jnp.stack([core, group_here, chip]).astype(jnp.int32)
    mine = join(pieces, from_chips(chunk))
    early, spread = lax.optimization_barrier((own_start(where, mine, swap_cores(mine), n), spread))
    source_pieces = deliver(spread, readers)
    own_rows, half3 = own_finish(where, early, stacked_left)
    half3, source_pieces = lax.optimization_barrier((half3, source_pieces))
    rotated = rotate_by_source(where, source_pieces, half3)
    return (own_rows.T[None], rotated[None])


def solution(mesh):
    sectors, groups = mesh.devices.shape
    fine = Mesh(mesh.devices.reshape(sectors, groups // 2, 2), ("sector", "x", "core"))
    ops = ("x", "core")
    return jax.shard_map(
        shards,
        mesh=fine,
        in_specs=(
            P("sector", None, None),
            P("sector", ops, None, None),
            P("sector", ops, None, None),
            P(ops, None),
            P(ops, "sector"),
        ),
        out_specs=(P("sector", None, ops), P("sector", ops, None, None)),
        check_vma=False,
    )
```
